512 devices in a mesh: seq: 32 (over z_hi, y, core), section: 16 (over z_lo, x).
Axes of the slice: x: 4, y: 4, z: 16 (z_hi: 4, z_lo: 4; z = z_hi * 4 + z_lo), core: 2. Of those that a mesh axis runs over, the one named last changes fastest.
Arguments:
- queries: bfloat16 [16, 2, 4096, 2048], P('section', None, 'seq'), may hold values from -120 to 120
- keys: bfloat16 [16, 2, 4096, 1024], P('section', None, 'seq'), may hold values from -4 to 4
- values: bfloat16 [16, 2, 4096, 1024], P('section', None, 'seq'), may hold values from -8 to 8
- out_grad: bfloat16 [16, 4096, 2048], P('section', 'seq'), may hold values from -6 to 6
- segments: int32 [2, 4096], replicated, may hold values from 0 to 3, never falling along the last dimension, each value on 1 to 2048 neighbouring positions
Outputs:
- attended: bfloat16 [16, 4096, 2048], P('section', 'seq')
- grad_queries: bfloat16 [16, 4096, 2048], P('section', 'seq')
- grad_keys: bfloat16 [16, 4096, 1024], P('section', 'seq')
- grad_values: bfloat16 [16, 4096, 1024], P('section', 'seq')
The draws below stay inside these ranges and needn't reach their ends.
Inputs may be any that keep to these rules, and one draw needn't show every extreme that they name: `segments`: documents are numbered in order along each micro-batch.
All inputs are finite; a program needn't handle non-finite values.
Results may differ from the reference program's by a relative error of at most 0.033.
Values may be sent and summed in bfloat16 or wider, within the bound.
A program may use at most 64 MiB of HBM per device.

```python
import math
import jax
import jax.numpy as jnp
import numpy as np
from jax import lax

QHEADS = 16
KVHEADS = 8
HEAD_DIM = 128
WINDOW = 256
SHARD_ROWS = 128
TOKENS = 4096
LAYERS = 16


def drawn_pair(key):
    base = jax.random.fold_in(key, 11)
    query_seed, key_seed = jax.random.split(base, 2)
    groups = QHEADS // KVHEADS
    key_raw = jnp.clip(jax.random.normal(key_seed, (LAYERS, 2, TOKENS, KVHEADS, HEAD_DIM), jnp.float32), -4.0, 4.0)
    query_raw = 2.3 * jnp.clip(jax.random.normal(query_seed, (LAYERS, 2, TOKENS, KVHEADS, groups, HEAD_DIM), jnp.float32), -4.0, 4.0)
    return (query_raw.reshape(LAYERS, 2, TOKENS, QHEADS * HEAD_DIM), key_raw.reshape(LAYERS, 2, TOKENS, KVHEADS * HEAD_DIM))


def draw_queries(key, part):
    return drawn_pair(key)[0].astype(jnp.bfloat16)


def draw_keys(key, part):
    return drawn_pair(key)[1].astype(jnp.bfloat16)


def steps_of(own_key, shape, shards, low, top_value):
    factor_of = 1.0
    for dim, blocks in shards:
        heights = jax.random.uniform(jax.random.fold_in(jax.random.fold_in(own_key, 6), dim), (blocks,), jnp.float32, low / len(shards), top_value / len(shards))
        factor_of = factor_of * jnp.repeat(jnp.exp(heights), shape[dim] // blocks).reshape((-1,) + (1,) * (len(shape) - 1 - dim))
    return factor_of


def profile(number_of, total, bound, skew):
    weights = [(1 << 20) // math.isqrt(rank ** skew) + 1 for rank in range(2, number_of + 1)]
    rest, counts = total - bound - (number_of - 1), [1] * (number_of - 1)
    while rest > 0:
        movable = [i for i in range(number_of - 1) if counts[i] < bound]
        pool, budget = sum([weights[i] for i in movable]), rest
        for i in movable:
            more = min(bound - counts[i], max(1, budget * weights[i] // pool), rest)
            counts[i] = counts[i] + more
            rest = rest - more
    return np.array([bound] + counts)


def ragged(own_key, number_of, total, limit, slope):
    if number_of == 2:
        one = jax.random.randint(own_key, (), max(1, total - limit), min(limit, total - 1) + 1)
        return jnp.stack([one, total - one])
    tallies = jnp.asarray(profile(number_of, total, limit, slope), jnp.int32)
    pairs = (number_of - 1) // 2
    donor, taker = tallies[1:1 + 2 * pairs:2], tallies[2:2 + 2 * pairs:2]
    slack = jnp.minimum(donor - 1, limit - taker)
    shifted = jax.random.randint(jax.random.fold_in(own_key, 1), (pairs,), 0, 1 << 20) % (slack + 1)
    tallies = tallies.at[1:1 + 2 * pairs:2].set(donor - shifted).at[2:2 + 2 * pairs:2].set(taker + shifted)
    return tallies[jax.random.permutation(jax.random.fold_in(own_key, 2), number_of)]


def scatter_about(rng, shape, scale, limit, cuts=(), held_as=jnp.bfloat16):
    factor_of = steps_of(rng, shape, cuts, -0.22, 0.18) if cuts else 1.0
    entries = jax.random.normal(rng, shape, jnp.float32) * scale * factor_of
    return jnp.minimum(jnp.maximum(entries, -limit), limit).astype(held_as)


def setup_inputs(seed: int = 0) -> dict:
    key_list = jax.random.split(jax.random.key(seed), 6)
    queries = draw_queries(jax.random.fold_in(key_list[5], 71), 0)
    keys = draw_keys(jax.random.fold_in(key_list[5], 71), 0)
    values = scatter_about(key_list[2], (LAYERS, 2, TOKENS, KVHEADS * HEAD_DIM), 2.0, 8.0, ((0, 16), (2, 32)))
    out_grad = scatter_about(key_list[3], (LAYERS, TOKENS, QHEADS * HEAD_DIM), 1.0, 6.0, ((0, 16), (1, 32)))
    segments = jax.vmap(lambda own: jnp.searchsorted(jnp.cumsum(ragged(own, 4, TOKENS, TOKENS // 2, 0)), jnp.arange(TOKENS), side="right"))(jax.random.split(key_list[4], 2)).reshape((2, TOKENS)).astype(jnp.int32)
    return dict(queries=queries, keys=keys, values=values, out_grad=out_grad, segments=segments)


score_scale = 168.0 ** -0.5
masked_score = -1.0e30


def masked_probs(query_block, key_span, seg_query, seg_key, query_pos, key_pos):
    row_count = query_block.shape[0]
    span_rows = key_span.shape[0]
    queries_grouped = query_block.astype(jnp.float32).reshape(row_count, KVHEADS, QHEADS // KVHEADS, HEAD_DIM)
    keys_grouped = key_span.astype(jnp.float32).reshape(span_rows, KVHEADS, HEAD_DIM)
    scores = jnp.einsum("rkgd,lkd->kgrl", queries_grouped, keys_grouped) * score_scale
    offset = query_pos[:, None] - key_pos[None, :]
    allowed = (seg_query[:, None] == seg_key[None, :]) & (offset >= 0) & (offset < WINDOW)
    scores = jnp.where(allowed, scores, masked_score)
    highest = jnp.max(scores, axis=-1, keepdims=True)
    weights = jnp.exp(scores - highest)
    return weights / jnp.sum(weights, axis=-1, keepdims=True)


def padded_inputs(key_all, value_all, seg_all):
    width = key_all.shape[1]
    key_pad = jnp.concatenate([jnp.zeros((WINDOW, width), key_all.dtype), key_all], axis=0)
    value_pad = jnp.concatenate([jnp.zeros((WINDOW, width), value_all.dtype), value_all], axis=0)
    seg_pad = jnp.concatenate([jnp.full((WINDOW,), -1, jnp.int32), seg_all.astype(jnp.int32)], axis=0)
    return key_pad, value_pad, seg_pad


def block_inputs(query_all, key_pad, value_pad, seg_pad, seg_all, block):
    row_start = (block * SHARD_ROWS).astype(jnp.int32)
    span_rows = WINDOW + SHARD_ROWS
    query_block = lax.dynamic_slice_in_dim(query_all, row_start, SHARD_ROWS, 0)
    key_span = lax.dynamic_slice_in_dim(key_pad, row_start, span_rows, 0)
    value_span = lax.dynamic_slice_in_dim(value_pad, row_start, span_rows, 0)
    seg_key = lax.dynamic_slice_in_dim(seg_pad, row_start, span_rows, 0)
    seg_query = lax.dynamic_slice_in_dim(seg_all.astype(jnp.int32), row_start, SHARD_ROWS, 0)
    query_pos = row_start + jnp.arange(SHARD_ROWS, dtype=jnp.int32)
    key_pos = row_start - WINDOW + jnp.arange(span_rows, dtype=jnp.int32)
    return row_start, query_block, key_span, value_span, seg_query, seg_key, query_pos, key_pos


def layer_forward(query_all, key_all, value_all, seg_all):
    key_pad, value_pad, seg_pad = padded_inputs(key_all, value_all, seg_all)

    def one_block(block):
        row_start, query_block, key_span, value_span, seg_query, seg_key, query_pos, key_pos = block_inputs(query_all, key_pad, value_pad, seg_pad, seg_all, block)
        probs = masked_probs(query_block, key_span, seg_query, seg_key, query_pos, key_pos)
        probs_half = lax.optimization_barrier(probs.astype(jnp.bfloat16)).astype(jnp.float32)
        values_grouped = value_span.astype(jnp.float32).reshape(WINDOW + SHARD_ROWS, KVHEADS, HEAD_DIM)
        output = jnp.einsum("kgrl,lkd->rkgd", probs_half, values_grouped)
        return output.reshape(SHARD_ROWS, QHEADS * HEAD_DIM).astype(jnp.bfloat16)

    blocks = lax.map(one_block, jnp.arange(TOKENS // SHARD_ROWS, dtype=jnp.int32))
    return blocks.reshape(TOKENS, QHEADS * HEAD_DIM)


def layer_backward(query_all, key_all, value_all, grad_all, seg_all):
    key_pad, value_pad, seg_pad = padded_inputs(key_all, value_all, seg_all)
    span_rows = WINDOW + SHARD_ROWS
    width = KVHEADS * HEAD_DIM
    groups = QHEADS // KVHEADS

    def one_block(carry, block):
        key_acc, value_acc = carry
        row_start, query_block, key_span, value_span, seg_query, seg_key, query_pos, key_pos = block_inputs(query_all, key_pad, value_pad, seg_pad, seg_all, block)
        probs = masked_probs(query_block, key_span, seg_query, seg_key, query_pos, key_pos)
        probs_half = lax.optimization_barrier(probs.astype(jnp.bfloat16)).astype(jnp.float32)
        values_grouped = value_span.astype(jnp.float32).reshape(span_rows, KVHEADS, HEAD_DIM)
        keys_grouped = key_span.astype(jnp.float32).reshape(span_rows, KVHEADS, HEAD_DIM)
        queries_grouped = query_block.astype(jnp.float32).reshape(SHARD_ROWS, KVHEADS, groups, HEAD_DIM)
        recomputed = jnp.einsum("kgrl,lkd->rkgd", probs_half, values_grouped)
        recomputed = lax.optimization_barrier(recomputed.astype(jnp.bfloat16)).astype(jnp.float32)
        grad_block = lax.dynamic_slice_in_dim(grad_all, row_start, SHARD_ROWS, 0)
        grad_grouped = grad_block.astype(jnp.float32).reshape(SHARD_ROWS, KVHEADS, groups, HEAD_DIM)
        grad_probs = jnp.einsum("rkgd,lkd->kgrl", grad_grouped, values_grouped)
        row_delta = jnp.sum(grad_grouped * recomputed, axis=-1).transpose(1, 2, 0)
        grad_scores = score_scale * probs * (grad_probs - row_delta[..., None])
        grad_scores = lax.optimization_barrier(grad_scores.astype(jnp.bfloat16)).astype(jnp.float32)
        query_grad = jnp.einsum("kgrl,lkd->rkgd", grad_scores, keys_grouped).reshape(SHARD_ROWS, QHEADS * HEAD_DIM).astype(jnp.bfloat16)
        key_terms = jnp.einsum("kgrl,rkgd->lkd", grad_scores, queries_grouped).reshape(span_rows, width)
        value_terms = jnp.einsum("kgrl,rkgd->lkd", probs_half, grad_grouped).reshape(span_rows, width)
        key_remote = lax.optimization_barrier(key_terms[:WINDOW].astype(jnp.bfloat16)).astype(jnp.float32)
        value_remote = lax.optimization_barrier(value_terms[:WINDOW].astype(jnp.bfloat16)).astype(jnp.float32)
        key_terms = jnp.concatenate([key_remote, key_terms[WINDOW:]], axis=0)
        value_terms = jnp.concatenate([value_remote, value_terms[WINDOW:]], axis=0)
        key_acc = lax.dynamic_update_slice_in_dim(key_acc, lax.dynamic_slice_in_dim(key_acc, row_start, span_rows, 0) + key_terms, row_start, 0)
        value_acc = lax.dynamic_update_slice_in_dim(value_acc, lax.dynamic_slice_in_dim(value_acc, row_start, span_rows, 0) + value_terms, row_start, 0)
        return (key_acc, value_acc), query_grad

    start_acc = (jnp.zeros((WINDOW + TOKENS, width), jnp.float32), jnp.zeros((WINDOW + TOKENS, width), jnp.float32))
    (key_acc, value_acc), query_blocks = lax.scan(one_block, start_acc, jnp.arange(TOKENS // SHARD_ROWS, dtype=jnp.int32))
    query_grad = query_blocks.reshape(TOKENS, QHEADS * HEAD_DIM)
    return query_grad, key_acc[WINDOW:].astype(jnp.bfloat16), value_acc[WINDOW:].astype(jnp.bfloat16)


def reference(queries, keys, values, out_grad, segments):
    def per_layer(layer_inputs):
        query_layer, key_layer, value_layer, grad_layer = layer_inputs
        attended = layer_forward(query_layer[0], key_layer[0], value_layer[0], segments[0])
        query_grad, key_grad, value_grad = layer_backward(query_layer[1], key_layer[1], value_layer[1], grad_layer, segments[1])
        return attended, query_grad, key_grad, value_grad

    results = lax.map(per_layer, (queries, keys, values, out_grad))
    return (jnp.roll(results[0], 1, axis=0), jnp.roll(results[1], -1, axis=0), jnp.roll(results[2], -1, axis=0), jnp.roll(results[3], -1, axis=0))
```

```python
import functools

import jax
import jax.numpy as jnp
from jax import lax
from jax.experimental import pallas as pl
from jax.experimental.pallas import tpu as pltpu
from jax.sharding import PartitionSpec as P

HEAD_DIM = 128
WINDOW = 256
ROWS = 128
COLUMNS = 4
PIECE = ROWS // COLUMNS
MESH = pl.DeviceIdType.MESH

score_scale = 168.0 ** (-0.5)
masked_score = -1e30

CHUNKS = ((1, 0), (1, 1), (0, 0), (0, 1))


def last_last(a, b):
    return lax.dot_general(a, b, (((1,), (1,)), ((), ())), preferred_element_type=jnp.float32)


def first_first(a, b):
    return lax.dot_general(a, b, (((0,), (0,)), ((), ())), preferred_element_type=jnp.float32)


def kernel(
    tops,
    sections,
    kv_heads,
    q_ref,
    k_ref,
    v_ref,
    do_ref,
    seg_ref,
    att_out,
    dq_out,
    dk_out,
    dv_out,
    span,
    bias,
    att,
    dq,
    near,
    far,
    own,
    mate_near,
    got,
    final,
    rel_a,
    rel_b,
    back_a,
    back_b,
    loc_sem,
    r_send,
    r_recv,
    a_send,
    a_recv,
    b_send,
    b_recv,
    c_send,
    c_recv,
    e_send,
    e_recv,
    f_send,
    f_recv,
    g_send,
    g_recv,
    ba_send,
    ba_recv,
    bb_send,
    bb_recv,
    bc_send,
    bc_recv,
    s_send,
    s_recv,
):
    me = lax.axis_index("seq")
    sec = lax.axis_index("section")
    core = lax.rem(me, 2)
    y = lax.rem(lax.div(me, 2), COLUMNS)
    top = lax.div(me, 2 * COLUMNS)
    last = COLUMNS - 1

    def at(top_of, y_of):
        return ((top_of * COLUMNS + y_of) * 2 + core, sec)

    mate = (me + 1 - 2 * core, sec)
    after = (me, lax.rem(sec + 1, sections))
    before = (me, lax.rem(sec + sections - 1, sections))
    has_next = top < tops - 1
    has_prev = top > 0

    def copy(src, dst, send, recv, device):
        return pltpu.make_async_remote_copy(
            src_ref=src,
            dst_ref=dst,
            send_sem=send,
            recv_sem=recv,
            device_id=device,
            device_id_type=MESH,
        )

    def arrived(dst, recv):
        copy(dst, dst, e_send.at[0], recv, mate).wait_recv()

    def sent(src, send):
        copy(src, src, send, e_recv.at[0], mate).wait_send()

    sources = (k_ref, v_ref)

    def piece(q):
        return pl.ds(q * PIECE, PIECE)

    @pl.when(me == 0)
    def _():
        span[:, :, 0:WINDOW, :] = jnp.zeros((2, 2, WINDOW, span.shape[3]), span.dtype)

    @pl.when(me == 1)
    def _():
        span[:, :, 0:ROWS, :] = jnp.zeros((2, 2, ROWS, span.shape[3]), span.dtype)

    @pl.when(me >= tops * 2 * COLUMNS - 2)
    def _():
        got[...] = jnp.zeros_like(got)

    for c, (m, kv) in enumerate(CHUNKS):
        pltpu.make_async_copy(
            sources[kv].at[m], span.at[kv, m, pl.ds(WINDOW, ROWS)], loc_sem.at[c]
        ).start()

    barrier = pltpu.get_barrier_semaphore()
    pl.semaphore_signal(barrier, inc=1, device_id=mate, device_id_type=MESH)
    pl.semaphore_signal(barrier, inc=1, device_id=after, device_id_type=MESH)
    pl.semaphore_signal(barrier, inc=1, device_id=before, device_id_type=MESH)
    for step in range(1, COLUMNS):
        pl.semaphore_signal(
            barrier,
            inc=1,
            device_id=at(top, lax.rem(y + step, COLUMNS)),
            device_id_type=MESH,
        )

    for step in (1, tops - 1):
        pl.semaphore_signal(
            barrier, inc=1, device_id=at(lax.rem(top + step, tops), y), device_id_type=MESH
        )

    column_of = lax.broadcasted_iota(jnp.int32, (ROWS, ROWS), 1)
    row_of = lax.broadcasted_iota(jnp.int32, (ROWS, ROWS), 0)
    for m in range(2):
        here = pl.ds(pl.multiple_of(me * ROWS, ROWS), ROWS)
        seg_query = jnp.broadcast_to(seg_ref[m : m + 1, here].astype(jnp.float32), (ROWS, ROWS))
        for part in range(3):
            block = jnp.maximum(me - 2 + part, 0)
            there = pl.ds(pl.multiple_of(block * ROWS, ROWS), ROWS)
            seg_key = jnp.broadcast_to(seg_ref[m : m + 1, there].astype(jnp.float32), (ROWS, ROWS)).T
            offset = column_of + WINDOW - part * ROWS - row_of
            allowed = (seg_query == seg_key) & (offset >= 0) & (offset < WINDOW)
            allowed = allowed & (row_of + (part - 2 + me) * ROWS >= 0)
            value = jnp.where(allowed, 0.0, masked_score)
            bias[m, part * ROWS : (part + 1) * ROWS, 0:ROWS] = value
            bias[m, part * ROWS : (part + 1) * ROWS, ROWS : 2 * ROWS] = value

    pl.semaphore_wait(barrier, 3 + COLUMNS - 1 + 2)

    def halo_b(c, src):
        m, kv = CHUNKS[c]

        @pl.when(y == 0)
        def _():
            copy(src, span.at[kv, m, piece(0)], b_send.at[c], b_recv.at[c], at(top + 1, y)).start()

        @pl.when(y > 0)
        def _():
            copy(src, rel_b.at[c], b_send.at[c], b_recv.at[c], at(top + 1, y)).start()

    crossing = (y == last) & has_next
    for c, (m, kv) in enumerate(CHUNKS):
        source = sources[kv].at[m]

        @pl.when(crossing)
        def _():
            for q in range(last):
                copy(
                    source.at[piece(q)], rel_a.at[c], a_send.at[c, q], a_recv.at[c], at(top, q)
                ).start()
            copy(
                source.at[piece(last)], rel_b.at[c], b_send.at[c], b_recv.at[c], at(top + 1, last)
            ).start()

        @pl.when(y < last)
        def _():
            copy(
                source,
                span.at[kv, m, pl.ds(0, ROWS)],
                r_send.at[c],
                r_recv.at[c],
                at(top, y + 1),
            ).start()

        @pl.when(core == 0)
        def _():
            copy(
                source, span.at[kv, m, pl.ds(ROWS, ROWS)], e_send.at[c], e_recv.at[c], mate
            ).start()

    def relay_b(c):
        @pl.when((y < last) & has_next)
        def _():
            arrived(rel_a.at[c], a_recv.at[c])
            halo_b(c, rel_a.at[c])

    def relay_c(c):
        m, kv = CHUNKS[c]

        @pl.when((y > 0) & has_prev)
        def _():
            arrived(rel_b.at[c], b_recv.at[c])
            for q in range(1, COLUMNS):

                @pl.when(y == q)
                def _():
                    copy(
                        rel_b.at[c],
                        span.at[kv, m, piece(q)],
                        c_send.at[c],
                        c_recv.at[c, q],
                        at(top, 0),
                    ).start()

        @pl.when((y == 0) & has_prev)
        def _():
            arrived(span.at[kv, m, piece(0)], b_recv.at[c])
            for q in range(1, COLUMNS):
                arrived(span.at[kv, m, piece(q)], c_recv.at[c, q])

        @pl.when(y > 0)
        def _():
            arrived(span.at[kv, m, pl.ds(0, ROWS)], r_recv.at[c])

        @pl.when((core == 1) & (me >= 2))
        def _():
            copy(
                span.at[kv, m, pl.ds(0, ROWS)],
                span.at[kv, m, pl.ds(ROWS, ROWS)],
                e_send.at[c],
                e_recv.at[c],
                mate,
            ).start()

    def span_ready(c):
        m, kv = CHUNKS[c]

        @pl.when(me > 0)
        def _():
            arrived(span.at[kv, m, pl.ds(ROWS, ROWS)], e_recv.at[c])

        pltpu.make_async_copy(
            sources[kv].at[m], span.at[kv, m, pl.ds(WINDOW, ROWS)], loc_sem.at[c]
        ).wait()

    def pair_of(ref, index, g):
        first = pl.multiple_of(g * 2 * HEAD_DIM, HEAD_DIM)
        second = pl.multiple_of(g * 2 * HEAD_DIM + HEAD_DIM, HEAD_DIM)
        return jnp.concatenate(
            [
                ref[index + (slice(None), pl.ds(first, HEAD_DIM))],
                ref[index + (slice(None), pl.ds(second, HEAD_DIM))],
            ],
            axis=0,
        )

    def store_pair(ref, g, value):
        first = pl.multiple_of(g * 2 * HEAD_DIM, HEAD_DIM)
        second = pl.multiple_of(g * 2 * HEAD_DIM + HEAD_DIM, HEAD_DIM)
        ref[:, pl.ds(first, HEAD_DIM)] = value[:ROWS].astype(ref.dtype)
        ref[:, pl.ds(second, HEAD_DIM)] = value[ROWS:].astype(ref.dtype)

    def probs_of(m, g):
        columns = pl.ds(pl.multiple_of(g * HEAD_DIM, HEAD_DIM), HEAD_DIM)
        keys = span[0, m, :, columns]
        values = span[1, m, :, columns]
        queries = pair_of(q_ref, (m,), g)
        scores = last_last(keys, queries) * score_scale + bias[m]
        weights = jnp.exp(scores - jnp.max(scores, axis=0, keepdims=True))
        probs = weights * (1.0 / jnp.sum(weights, axis=0, keepdims=True))
        return keys, values, queries, probs

    def backward(g, carry):
        keys, values, queries, probs = probs_of(1, g)
        columns = pl.ds(pl.multiple_of(g * HEAD_DIM, HEAD_DIM), HEAD_DIM)
        grads = pair_of(do_ref, (), g)
        half = probs.astype(jnp.bfloat16)
        grad_probs = last_last(values, grads)
        delta = jnp.sum(probs * grad_probs, axis=0, keepdims=True)
        grad_scores = (probs * score_scale * (grad_probs - delta)).astype(jnp.bfloat16)
        store_pair(dq, g, first_first(grad_scores, keys))
        for kv, terms in enumerate(
            (
                jnp.dot(grad_scores, queries, preferred_element_type=jnp.float32),
                jnp.dot(half, grads, preferred_element_type=jnp.float32),
            )
        ):
            far[kv, :, columns] = terms[0:ROWS].astype(jnp.bfloat16)
            near[kv, :, columns] = terms[ROWS:WINDOW].astype(jnp.bfloat16)
            own[kv, :, columns] = terms[WINDOW:]
        return carry

    def forward(g, carry):
        _, values, _, probs = probs_of(0, g)
        store_pair(att, g, first_first(probs.astype(jnp.bfloat16), values))
        return carry

    for c in range(4):
        relay_b(c)
    for c in range(2):
        relay_c(c)
    for c in range(2):
        span_ready(c)
    lax.fori_loop(0, kv_heads, backward, 0)

    for kv in range(2):
        copy(near.at[kv], mate_near.at[kv], f_send.at[kv], f_recv.at[kv], mate).start()
    copy(dq, dq_out, s_send.at[1], s_recv.at[1], before).start()
    for c in range(2, 4):
        relay_c(c)

    back_crossing = (y == 0) & has_prev

    def back_b_send(kv, src):
        @pl.when(y == last)
        def _():
            copy(
                src, got.at[kv, piece(last)], bb_send.at[kv], bb_recv.at[kv], at(top - 1, y)
            ).start()

        @pl.when(y < last)
        def _():
            copy(src, back_b.at[kv], bb_send.at[kv], bb_recv.at[kv], at(top - 1, y)).start()

    for kv in range(2):
        arrived(mate_near.at[kv], f_recv.at[kv])

        @pl.when(core == 1)
        def _():
            far[kv] = (
                far[kv].astype(jnp.float32) + mate_near[kv].astype(jnp.float32)
            ).astype(jnp.bfloat16)

        @pl.when(y > 0)
        def _():
            copy(far.at[kv], got.at[kv], g_send.at[kv], g_recv.at[kv], at(top, y - 1)).start()

        @pl.when(back_crossing)
        def _():
            for q in range(1, COLUMNS):
                copy(
                    far.at[kv, piece(q)],
                    back_a.at[kv],
                    ba_send.at[kv, q],
                    ba_recv.at[kv],
                    at(top, q),
                ).start()
            copy(
                far.at[kv, piece(0)], back_b.at[kv], bb_send.at[kv], bb_recv.at[kv], at(top - 1, 0)
            ).start()

    for kv in range(2):

        @pl.when((y > 0) & has_prev)
        def _():
            arrived(back_a.at[kv], ba_recv.at[kv])
            back_b_send(kv, back_a.at[kv])

    for c in range(2, 4):
        span_ready(c)
    lax.fori_loop(0, kv_heads, forward, 0)
    copy(att, att_out, s_send.at[0], s_recv.at[0], after).start()

    for kv in range(2):

        @pl.when((y < last) & has_next)
        def _():
            arrived(back_b.at[kv], bb_recv.at[kv])
            for q in range(last):

                @pl.when(y == q)
                def _():
                    copy(
                        back_b.at[kv],
                        got.at[kv, piece(q)],
                        bc_send.at[kv],
                        bc_recv.at[kv, q],
                        at(top, last),
                    ).start()

    outs = (dk_out, dv_out)
    for kv in range(2):

        @pl.when(y < last)
        def _():
            arrived(got.at[kv], g_recv.at[kv])

        @pl.when((y == last) & has_next)
        def _():
            arrived(got.at[kv, piece(last)], bb_recv.at[kv])
            for q in range(last):
                arrived(got.at[kv, piece(q)], bc_recv.at[kv, q])

        @pl.when(core == 0)
        def _():
            final[kv] = (
                own[kv] + mate_near[kv].astype(jnp.float32) + got[kv].astype(jnp.float32)
            ).astype(jnp.bfloat16)

        @pl.when(core == 1)
        def _():
            final[kv] = (own[kv] + got[kv].astype(jnp.float32)).astype(jnp.bfloat16)

        copy(final.at[kv], outs[kv], s_send.at[2 + kv], s_recv.at[2 + kv], before).start()

    for c, (m, kv) in enumerate(CHUNKS):
        source = sources[kv].at[m]

        @pl.when(crossing)
        def _():
            for q in range(last):
                sent(source.at[piece(q)], a_send.at[c, q])

        @pl.when(has_next)
        def _():
            sent(rel_a.at[c], b_send.at[c])

        @pl.when(y < last)
        def _():
            sent(source, r_send.at[c])

        @pl.when((y > 0) & has_prev)
        def _():
            sent(rel_b.at[c], c_send.at[c])

        @pl.when((core == 0) | (me >= 2))
        def _():
            sent(source, e_send.at[c])

    for kv in range(2):
        sent(near.at[kv], f_send.at[kv])

        @pl.when(y > 0)
        def _():
            sent(far.at[kv], g_send.at[kv])

        @pl.when(back_crossing)
        def _():
            for q in range(1, COLUMNS):
                sent(far.at[kv, piece(q)], ba_send.at[kv, q])

        @pl.when(has_prev)
        def _():
            sent(back_a.at[kv], bb_send.at[kv])

        @pl.when((y < last) & has_next)
        def _():
            sent(back_b.at[kv], bc_send.at[kv])

    for i, (src, dst) in enumerate(
        ((att, att_out), (dq, dq_out), (final.at[0], dk_out), (final.at[1], dv_out))
    ):
        sent(src, s_send.at[i])
        arrived(dst, s_recv.at[i])


def shards(tops, sections, queries, keys, values, out_grad, segments):
    q_width = queries.shape[-1]
    k_width = keys.shape[-1]
    kv_heads = k_width // HEAD_DIM
    half, full = jnp.bfloat16, jnp.float32
    vmem = pl.BlockSpec(memory_space=pltpu.VMEM)
    hbm = pl.BlockSpec(memory_space=pl.ANY)
    dma = pltpu.SemaphoreType.DMA
    pair_sems = [dma((2,))] * 2
    results = pl.pallas_call(
        functools.partial(kernel, tops, sections, kv_heads),
        out_shape=[
            jax.ShapeDtypeStruct((ROWS, q_width), half),
            jax.ShapeDtypeStruct((ROWS, q_width), half),
            jax.ShapeDtypeStruct((ROWS, k_width), half),
            jax.ShapeDtypeStruct((ROWS, k_width), half),
        ],
        in_specs=[vmem, hbm, hbm, vmem, vmem],
        out_specs=[hbm] * 4,
        scratch_shapes=[
            pltpu.VMEM((2, 2, WINDOW + ROWS, k_width), half),
            pltpu.VMEM((2, WINDOW + ROWS, 2 * ROWS), full),
            pltpu.VMEM((ROWS, q_width), half),
            pltpu.VMEM((ROWS, q_width), half),
            pltpu.VMEM((2, ROWS, k_width), half),
            pltpu.VMEM((2, ROWS, k_width), half),
            pltpu.VMEM((2, ROWS, k_width), full),
            pltpu.VMEM((2, ROWS, k_width), half),
            pltpu.VMEM((2, ROWS, k_width), half),
            pltpu.VMEM((2, ROWS, k_width), half),
            pltpu.VMEM((4, PIECE, k_width), half),
            pltpu.VMEM((4, PIECE, k_width), half),
            pltpu.VMEM((2, PIECE, k_width), half),
            pltpu.VMEM((2, PIECE, k_width), half),
            dma((4,)),
            dma((4,)),
            dma((4,)),
            dma((4, COLUMNS)),
            dma((4,)),
            dma((4,)),
            dma((4,)),
            dma((4,)),
            dma((4, COLUMNS)),
            dma((4,)),
            dma((4,)),
            *pair_sems,
            *pair_sems,
            dma((2, COLUMNS)),
            dma((2,)),
            *pair_sems,
            dma((2,)),
            dma((2, COLUMNS)),
            dma((4,)),
            dma((4,)),
        ],
        compiler_params=pltpu.CompilerParams(collective_id=0, has_side_effects=True),
    )(queries[0], keys[0], values[0], out_grad[0], segments)
    return tuple(result[None] for result in results)


def solution(mesh):
    tops = mesh.shape["seq"] // (2 * COLUMNS)
    sections = mesh.shape["section"]
    return jax.shard_map(
        functools.partial(shards, tops, sections),
        mesh=mesh,
        in_specs=(
            P("section", None, "seq", None),
            P("section", None, "seq", None),
            P("section", None, "seq", None),
            P("section", "seq", None),
            P(),
        ),
        out_specs=(
            P("section", "seq", None),
            P("section", "seq", None),
            P("section", "seq", None),
            P("section", "seq", None),
        ),
        check_vma=False,
    )
```

```python
import functools

import jax
import jax.numpy as jnp
from jax import lax
from jax.experimental import pallas as pl
from jax.experimental.pallas import tpu as pltpu
from jax.sharding import PartitionSpec as P

HEAD_DIM = 128
WINDOW = 256
ROWS = 128
COLUMNS = 4
PIECE = ROWS // COLUMNS
MESH = pl.DeviceIdType.MESH

score_scale = 168.0 ** (-0.5)
masked_score = -1e30

CHUNKS = tuple((m, h, kv) for m in (1, 0) for h in range(2) for kv in range(2))
TERMS = tuple((h, kv) for h in range(2) for kv in range(2))


def last_last(a, b):
    return lax.dot_general(a, b, (((1,), (1,)), ((), ())), preferred_element_type=jnp.float32)


def first_first(a, b):
    return lax.dot_general(a, b, (((0,), (0,)), ((), ())), preferred_element_type=jnp.float32)


def kernel(
    tops,
    sections,
    kv_heads,
    q_ref,
    k_ref,
    v_ref,
    do_ref,
    seg_ref,
    att_out,
    dq_out,
    dk_out,
    dv_out,
    span,
    bias,
    att,
    dq,
    near,
    far,
    own,
    mate_near,
    got,
    final,
    rel_a,
    rel_b,
    back_a,
    back_b,
    loc_sem,
    r_send,
    r_recv,
    a_send,
    a_recv,
    b_send,
    b_recv,
    c_send,
    c_recv,
    e_send,
    e_recv,
    f_send,
    f_recv,
    g_send,
    g_recv,
    ba_send,
    ba_recv,
    bb_send,
    bb_recv,
    bc_send,
    bc_recv,
    s_send,
    s_recv,
):
    me = lax.axis_index("seq")
    sec = lax.axis_index("section")
    core = lax.rem(me, 2)
    y = lax.rem(lax.div(me, 2), COLUMNS)
    top = lax.div(me, 2 * COLUMNS)
    last = COLUMNS - 1

    def at(top_of, y_of):
        return ((top_of * COLUMNS + y_of) * 2 + core, sec)

    mate = (me + 1 - 2 * core, sec)
    after = (me, lax.rem(sec + 1, sections))
    before = (me, lax.rem(sec + sections - 1, sections))
    has_next = top < tops - 1
    has_prev = top > 0

    def copy(src, dst, send, recv, device):
        return pltpu.make_async_remote_copy(
            src_ref=src,
            dst_ref=dst,
            send_sem=send,
            recv_sem=recv,
            device_id=device,
            device_id_type=MESH,
        )

    def arrived(dst, recv):
        copy(dst, dst, e_send.at[0], recv, mate).wait_recv()

    def sent(src, send):
        copy(src, src, send, e_recv.at[0], mate).wait_send()

    sources = (k_ref, v_ref)
    wide = k_ref.shape[-1] // 2
    all_rows = pl.ds(0, ROWS)
    near_rows = pl.ds(ROWS, ROWS)

    def piece(q):
        return pl.ds(q * PIECE, PIECE)

    def half(h):
        return pl.ds(h * wide, wide)

    def source(c, rows):
        m, h, kv = CHUNKS[c]
        return sources[kv].at[m, rows, half(h)]

    def spot(c, rows):
        m, h, kv = CHUNKS[c]
        return span.at[kv, m, rows, half(h)]

    def terms_at(ref, t, rows):
        h, kv = TERMS[t]
        return ref.at[kv, rows, half(h)]

    def loads(m, kv):
        return pltpu.make_async_copy(
            sources[kv].at[m], span.at[kv, m, pl.ds(WINDOW, ROWS)], loc_sem.at[m * 2 + kv]
        )

    @pl.when(me == 0)
    def _():
        span[:, :, 0:WINDOW, :] = jnp.zeros((2, 2, WINDOW, span.shape[3]), span.dtype)

    @pl.when(me == 1)
    def _():
        span[:, :, 0:ROWS, :] = jnp.zeros((2, 2, ROWS, span.shape[3]), span.dtype)

    @pl.when(me >= tops * 2 * COLUMNS - 2)
    def _():
        got[...] = jnp.zeros_like(got)

    for m in (1, 0):
        for kv in range(2):
            loads(m, kv).start()

    barrier = pltpu.get_barrier_semaphore()
    pl.semaphore_signal(barrier, inc=1, device_id=mate, device_id_type=MESH)
    pl.semaphore_signal(barrier, inc=1, device_id=after, device_id_type=MESH)
    pl.semaphore_signal(barrier, inc=1, device_id=before, device_id_type=MESH)
    for step in range(1, COLUMNS):
        pl.semaphore_signal(
            barrier,
            inc=1,
            device_id=at(top, lax.rem(y + step, COLUMNS)),
            device_id_type=MESH,
        )

    for step in (1, tops - 1):
        pl.semaphore_signal(
            barrier, inc=1, device_id=at(lax.rem(top + step, tops), y), device_id_type=MESH
        )

    column_of = lax.broadcasted_iota(jnp.int32, (ROWS, ROWS), 1)
    row_of = lax.broadcasted_iota(jnp.int32, (ROWS, ROWS), 0)
    for m in range(2):
        here = pl.ds(pl.multiple_of(me * ROWS, ROWS), ROWS)
        seg_query = jnp.broadcast_to(seg_ref[m : m + 1, here].astype(jnp.float32), (ROWS, ROWS))
        for part in range(3):
            block = jnp.maximum(me - 2 + part, 0)
            there = pl.ds(pl.multiple_of(block * ROWS, ROWS), ROWS)
            seg_key = jnp.broadcast_to(seg_ref[m : m + 1, there].astype(jnp.float32), (ROWS, ROWS)).T
            offset = column_of + WINDOW - part * ROWS - row_of
            allowed = (seg_query == seg_key) & (offset >= 0) & (offset < WINDOW)
            allowed = allowed & (row_of + (part - 2 + me) * ROWS >= 0)
            value = jnp.where(allowed, 0.0, masked_score)
            bias[m, part * ROWS : (part + 1) * ROWS, 0:ROWS] = value
            bias[m, part * ROWS : (part + 1) * ROWS, ROWS : 2 * ROWS] = value

    pl.semaphore_wait(barrier, 3 + COLUMNS - 1 + 2)

    def halo_b(c, src):
        @pl.when(y == 0)
        def _():
            copy(src, spot(c, piece(0)), b_send.at[c], b_recv.at[c], at(top + 1, y)).start()

        @pl.when(y > 0)
        def _():
            copy(src, rel_b.at[c], b_send.at[c], b_recv.at[c], at(top + 1, y)).start()

    crossing = (y == last) & has_next
    for c in range(len(CHUNKS)):

        @pl.when(crossing)
        def _():
            for q in range(last):
                copy(
                    source(c, piece(q)), rel_a.at[c], a_send.at[c, q], a_recv.at[c], at(top, q)
                ).start()
            copy(
                source(c, piece(last)), rel_b.at[c], b_send.at[c], b_recv.at[c], at(top + 1, last)
            ).start()

        @pl.when(y < last)
        def _():
            copy(
                source(c, all_rows), spot(c, all_rows), r_send.at[c], r_recv.at[c], at(top, y + 1)
            ).start()

        @pl.when(core == 0)
        def _():
            copy(
                source(c, all_rows), spot(c, near_rows), e_send.at[c], e_recv.at[c], mate
            ).start()

    def relay_b(c):
        @pl.when((y < last) & has_next)
        def _():
            arrived(rel_a.at[c], a_recv.at[c])
            halo_b(c, rel_a.at[c])

    def relay_c(c):
        @pl.when((y > 0) & has_prev)
        def _():
            arrived(rel_b.at[c], b_recv.at[c])
            for q in range(1, COLUMNS):

                @pl.when(y == q)
                def _():
                    copy(
                        rel_b.at[c], spot(c, piece(q)), c_send.at[c], c_recv.at[c, q], at(top, 0)
                    ).start()

    def pass_on(c):
        @pl.when((y == 0) & has_prev)
        def _():
            arrived(spot(c, piece(0)), b_recv.at[c])
            for q in range(1, COLUMNS):
                arrived(spot(c, piece(q)), c_recv.at[c, q])

        @pl.when(y > 0)
        def _():
            arrived(spot(c, all_rows), r_recv.at[c])

        @pl.when((core == 1) & (me >= 2))
        def _():
            copy(
                spot(c, all_rows), spot(c, near_rows), e_send.at[c], e_recv.at[c], mate
            ).start()

    def span_ready(c):
        m, h, kv = CHUNKS[c]

        @pl.when(me > 0)
        def _():
            arrived(spot(c, near_rows), e_recv.at[c])

        if h == 0:
            loads(m, kv).wait()

    def pair_of(ref, index, g):
        first = pl.multiple_of(g * 2 * HEAD_DIM, HEAD_DIM)
        second = pl.multiple_of(g * 2 * HEAD_DIM + HEAD_DIM, HEAD_DIM)
        return jnp.concatenate(
            [
                ref[index + (slice(None), pl.ds(first, HEAD_DIM))],
                ref[index + (slice(None), pl.ds(second, HEAD_DIM))],
            ],
            axis=0,
        )

    def store_pair(ref, g, value):
        first = pl.multiple_of(g * 2 * HEAD_DIM, HEAD_DIM)
        second = pl.multiple_of(g * 2 * HEAD_DIM + HEAD_DIM, HEAD_DIM)
        ref[:, pl.ds(first, HEAD_DIM)] = value[:ROWS].astype(ref.dtype)
        ref[:, pl.ds(second, HEAD_DIM)] = value[ROWS:].astype(ref.dtype)

    def probs_of(m, g):
        columns = pl.ds(pl.multiple_of(g * HEAD_DIM, HEAD_DIM), HEAD_DIM)
        keys = span[0, m, :, columns]
        values = span[1, m, :, columns]
        queries = pair_of(q_ref, (m,), g)
        scores = last_last(keys, queries) * score_scale + bias[m]
        weights = jnp.exp(scores - jnp.max(scores, axis=0, keepdims=True))
        probs = weights * (1.0 / jnp.sum(weights, axis=0, keepdims=True))
        return keys, values, queries, probs

    def backward(g, carry):
        keys, values, queries, probs = probs_of(1, g)
        columns = pl.ds(pl.multiple_of(g * HEAD_DIM, HEAD_DIM), HEAD_DIM)
        grads = pair_of(do_ref, (), g)
        rounded = probs.astype(jnp.bfloat16)
        grad_probs = last_last(values, grads)
        delta = jnp.sum(probs * grad_probs, axis=0, keepdims=True)
        grad_scores = (probs * score_scale * (grad_probs - delta)).astype(jnp.bfloat16)
        store_pair(dq, g, first_first(grad_scores, keys))
        for kv, terms in enumerate(
            (
                jnp.dot(grad_scores, queries, preferred_element_type=jnp.float32),
                jnp.dot(rounded, grads, preferred_element_type=jnp.float32),
            )
        ):
            far[kv, :, columns] = terms[0:ROWS].astype(jnp.bfloat16)
            near[kv, :, columns] = terms[ROWS:WINDOW].astype(jnp.bfloat16)
            own[kv, :, columns] = terms[WINDOW:]
        return carry

    def forward(g, carry):
        _, values, _, probs = probs_of(0, g)
        store_pair(att, g, first_first(probs.astype(jnp.bfloat16), values))
        return carry

    q_wide = q_ref.shape[-1] // 2
    half_heads = kv_heads // 2

    def q_half(ref, h):
        return ref.at[:, pl.ds(h * q_wide, q_wide)]

    def send_near(h):
        for kv in range(2):
            t = h * 2 + kv
            copy(
                terms_at(near, t, all_rows),
                terms_at(mate_near, t, all_rows),
                f_send.at[t],
                f_recv.at[t],
                mate,
            ).start()

    def send_queries(h):
        copy(q_half(dq, h), q_half(dq_out, h), s_send.at[2 + h], s_recv.at[2 + h], before).start()

    def send_attended(h):
        copy(q_half(att, h), q_half(att_out, h), s_send.at[h], s_recv.at[h], after).start()

    back_crossing = (y == 0) & has_prev

    def send_far(t):
        h, kv = TERMS[t]
        arrived(terms_at(mate_near, t, all_rows), f_recv.at[t])

        @pl.when(core == 1)
        def _():
            lanes = slice(h * wide, (h + 1) * wide)
            far[kv, :, lanes] = (
                far[kv, :, lanes].astype(jnp.float32)
                + mate_near[kv, :, lanes].astype(jnp.float32)
            ).astype(jnp.bfloat16)

        @pl.when(y > 0)
        def _():
            copy(
                terms_at(far, t, all_rows),
                terms_at(got, t, all_rows),
                g_send.at[t],
                g_recv.at[t],
                at(top, y - 1),
            ).start()

        @pl.when(back_crossing)
        def _():
            for q in range(1, COLUMNS):
                copy(
                    terms_at(far, t, piece(q)),
                    back_a.at[t],
                    ba_send.at[t, q],
                    ba_recv.at[t],
                    at(top, q),
                ).start()
            copy(
                terms_at(far, t, piece(0)),
                back_b.at[t],
                bb_send.at[t],
                bb_recv.at[t],
                at(top - 1, 0),
            ).start()

    def relay_back_b(t):
        @pl.when((y > 0) & has_prev)
        def _():
            arrived(back_a.at[t], ba_recv.at[t])

            @pl.when(y == last)
            def _():
                copy(
                    back_a.at[t],
                    terms_at(got, t, piece(last)),
                    bb_send.at[t],
                    bb_recv.at[t],
                    at(top - 1, y),
                ).start()

            @pl.when(y < last)
            def _():
                copy(
                    back_a.at[t], back_b.at[t], bb_send.at[t], bb_recv.at[t], at(top - 1, y)
                ).start()

    def relay_back_c(t):
        @pl.when((y < last) & has_next)
        def _():
            arrived(back_b.at[t], bb_recv.at[t])
            for q in range(last):

                @pl.when(y == q)
                def _():
                    copy(
                        back_b.at[t],
                        terms_at(got, t, piece(q)),
                        bc_send.at[t],
                        bc_recv.at[t, q],
                        at(top, last),
                    ).start()

    outs = (dk_out, dv_out)

    def finish(t):
        h, kv = TERMS[t]
        lanes = slice(h * wide, (h + 1) * wide)

        @pl.when(y < last)
        def _():
            arrived(terms_at(got, t, all_rows), g_recv.at[t])

        @pl.when((y == last) & has_next)
        def _():
            arrived(terms_at(got, t, piece(last)), bb_recv.at[t])
            for q in range(last):
                arrived(terms_at(got, t, piece(q)), bc_recv.at[t, q])

        total = own[kv, :, lanes] + got[kv, :, lanes].astype(jnp.float32)

        @pl.when(core == 0)
        def _():
            final[kv, :, lanes] = (total + mate_near[kv, :, lanes].astype(jnp.float32)).astype(
                jnp.bfloat16
            )

        @pl.when(core == 1)
        def _():
            final[kv, :, lanes] = total.astype(jnp.bfloat16)

        copy(
            terms_at(final, t, all_rows),
            outs[kv].at[:, half(h)],
            s_send.at[4 + t],
            s_recv.at[4 + t],
            before,
        ).start()

    for c in range(8):
        relay_b(c)
    for c in (0, 1):
        relay_c(c)
    for c in (0, 1):
        pass_on(c)
    for c in (0, 1):
        span_ready(c)
    lax.fori_loop(0, half_heads, backward, 0)
    send_near(0)
    send_queries(0)
    for c in (2, 3):
        relay_c(c)
    for c in (2, 3):
        pass_on(c)
    for t in (0, 1):
        send_far(t)
    for c in (2, 3):
        span_ready(c)
    lax.fori_loop(half_heads, kv_heads, backward, 0)
    send_near(1)
    send_queries(1)
    for t in (0, 1):
        relay_back_b(t)
    for t in (2, 3):
        send_far(t)
    for c in (4, 5):
        relay_c(c)
    for t in (2, 3):
        relay_back_b(t)
    for c in (6, 7):
        relay_c(c)
    for c in (4, 5):
        pass_on(c)
    for c in (4, 5):
        span_ready(c)
    lax.fori_loop(0, half_heads, forward, 0)
    send_attended(0)
    for t in (0, 1):
        relay_back_c(t)
    for c in (6, 7):
        pass_on(c)
    for c in (6, 7):
        span_ready(c)
    lax.fori_loop(half_heads, kv_heads, forward, 0)
    send_attended(1)
    for t in (2, 3):
        relay_back_c(t)
    for t in range(4):
        finish(t)

    for c in range(len(CHUNKS)):

        @pl.when(crossing)
        def _():
            for q in range(last):
                sent(source(c, piece(q)), a_send.at[c, q])

        @pl.when(has_next)
        def _():
            sent(rel_a.at[c], b_send.at[c])

        @pl.when(y < last)
        def _():
            sent(source(c, all_rows), r_send.at[c])

        @pl.when((y > 0) & has_prev)
        def _():
            sent(rel_b.at[c], c_send.at[c])

        @pl.when((core == 0) | (me >= 2))
        def _():
            sent(source(c, all_rows), e_send.at[c])

    for t in range(len(TERMS)):
        sent(terms_at(near, t, all_rows), f_send.at[t])

        @pl.when(y > 0)
        def _():
            sent(terms_at(far, t, all_rows), g_send.at[t])

        @pl.when(back_crossing)
        def _():
            for q in range(1, COLUMNS):
                sent(terms_at(far, t, piece(q)), ba_send.at[t, q])

        @pl.when(has_prev)
        def _():
            sent(back_a.at[t], bb_send.at[t])

        @pl.when((y < last) & has_next)
        def _():
            sent(back_b.at[t], bc_send.at[t])

    moved = [(q_half(att, h), q_half(att_out, h)) for h in range(2)]
    moved += [(q_half(dq, h), q_half(dq_out, h)) for h in range(2)]
    moved += [(terms_at(final, t, all_rows), outs[t % 2].at[:, half(t // 2)]) for t in range(4)]
    for i, (src, dst) in enumerate(moved):
        sent(src, s_send.at[i])
        arrived(dst, s_recv.at[i])


def shards(tops, sections, queries, keys, values, out_grad, segments):
    q_width = queries.shape[-1]
    k_width = keys.shape[-1]
    kv_heads = k_width // HEAD_DIM
    half, full = jnp.bfloat16, jnp.float32
    vmem = pl.BlockSpec(memory_space=pltpu.VMEM)
    hbm = pl.BlockSpec(memory_space=pl.ANY)
    dma = pltpu.SemaphoreType.DMA
    results = pl.pallas_call(
        functools.partial(kernel, tops, sections, kv_heads),
        out_shape=[
            jax.ShapeDtypeStruct((ROWS, q_width), half),
            jax.ShapeDtypeStruct((ROWS, q_width), half),
            jax.ShapeDtypeStruct((ROWS, k_width), half),
            jax.ShapeDtypeStruct((ROWS, k_width), half),
        ],
        in_specs=[vmem, hbm, hbm, vmem, vmem],
        out_specs=[hbm] * 4,
        scratch_shapes=[
            pltpu.VMEM((2, 2, WINDOW + ROWS, k_width), half),
            pltpu.VMEM((2, WINDOW + ROWS, 2 * ROWS), full),
            pltpu.VMEM((ROWS, q_width), half),
            pltpu.VMEM((ROWS, q_width), half),
            pltpu.VMEM((2, ROWS, k_width), half),
            pltpu.VMEM((2, ROWS, k_width), half),
            pltpu.VMEM((2, ROWS, k_width), full),
            pltpu.VMEM((2, ROWS, k_width), half),
            pltpu.VMEM((2, ROWS, k_width), half),
            pltpu.VMEM((2, ROWS, k_width), half),
            pltpu.VMEM((8, PIECE, k_width // 2), half),
            pltpu.VMEM((8, PIECE, k_width // 2), half),
            pltpu.VMEM((4, PIECE, k_width // 2), half),
            pltpu.VMEM((4, PIECE, k_width // 2), half),
            dma((4,)),
            dma((8,)),
            dma((8,)),
            dma((8, COLUMNS)),
            dma((8,)),
            dma((8,)),
            dma((8,)),
            dma((8,)),
            dma((8, COLUMNS)),
            dma((8,)),
            dma((8,)),
            dma((4,)),
            dma((4,)),
            dma((4,)),
            dma((4,)),
            dma((4, COLUMNS)),
            dma((4,)),
            dma((4,)),
            dma((4,)),
            dma((4,)),
            dma((4, COLUMNS)),
            dma((8,)),
            dma((8,)),
        ],
        compiler_params=pltpu.CompilerParams(collective_id=0, has_side_effects=True),
    )(queries[0], keys[0], values[0], out_grad[0], segments)
    return tuple(result[None] for result in results)


def solution(mesh):
    tops = mesh.shape["seq"] // (2 * COLUMNS)
    sections = mesh.shape["section"]
    return jax.shard_map(
        functools.partial(shards, tops, sections),
        mesh=mesh,
        in_specs=(
            P("section", None, "seq", None),
            P("section", None, "seq", None),
            P("section", None, "seq", None),
            P("section", "seq", None),
            P(),
        ),
        out_specs=(
            P("section", "seq", None),
            P("section", "seq", None),
            P("section", "seq", None),
            P("section", "seq", None),
        ),
        check_vma=False,
    )
```

```python
import functools

import jax
import jax.numpy as jnp
from jax import lax
from jax.experimental import pallas as pl
from jax.experimental.pallas import tpu as pltpu
from jax.sharding import PartitionSpec as P

HEAD_DIM = 128
WINDOW = 256
ROWS = 128
COLUMNS = 4
PIECE = ROWS // COLUMNS
MESH = pl.DeviceIdType.MESH

score_scale = 168.0 ** (-0.5)
masked_score = -1e30

CHUNKS = tuple((m, h, kv) for m in (1, 0) for h in range(2) for kv in range(2))
TERMS = tuple((h, kv) for h in range(2) for kv in range(2))


def last_last(a, b):
    return lax.dot_general(a, b, (((1,), (1,)), ((), ())), preferred_element_type=jnp.float32)


def first_first(a, b):
    return lax.dot_general(a, b, (((0,), (0,)), ((), ())), preferred_element_type=jnp.float32)


def kernel(
    tops,
    sections,
    kv_heads,
    q_ref,
    k_ref,
    v_ref,
    do_ref,
    seg_ref,
    att_out,
    dq_out,
    dk_out,
    dv_out,
    span,
    bias,
    att,
    dq,
    near,
    far,
    own,
    mate_near,
    got,
    final,
    rel_a,
    rel_b,
    back_a,
    back_b,
    loc_sem,
    r_send,
    r_recv,
    a_send,
    a_recv,
    b_send,
    b_recv,
    c_send,
    c_recv,
    e_send,
    e_recv,
    f_send,
    f_recv,
    g_send,
    g_recv,
    ba_send,
    ba_recv,
    bb_send,
    bb_recv,
    bc_send,
    bc_recv,
    s_send,
    s_recv,
):
    me = lax.axis_index("seq")
    sec = lax.axis_index("section")
    core = lax.rem(me, 2)
    y = lax.rem(lax.div(me, 2), COLUMNS)
    top = lax.div(me, 2 * COLUMNS)
    last = COLUMNS - 1

    def at(top_of, y_of):
        return ((top_of * COLUMNS + y_of) * 2 + core, sec)

    mate = (me + 1 - 2 * core, sec)
    after = (me, lax.rem(sec + 1, sections))
    before = (me, lax.rem(sec + sections - 1, sections))
    has_next = top < tops - 1
    has_prev = top > 0

    def copy(src, dst, send, recv, device):
        return pltpu.make_async_remote_copy(
            src_ref=src,
            dst_ref=dst,
            send_sem=send,
            recv_sem=recv,
            device_id=device,
            device_id_type=MESH,
        )

    def arrived(dst, recv):
        copy(dst, dst, e_send.at[0], recv, mate).wait_recv()

    def sent(src, send):
        copy(src, src, send, e_recv.at[0], mate).wait_send()

    sources = (k_ref, v_ref)
    wide = k_ref.shape[-1] // 2
    all_rows = pl.ds(0, ROWS)
    near_rows = pl.ds(ROWS, ROWS)

    def piece(q):
        return pl.ds(q * PIECE, PIECE)

    def half(h):
        return pl.ds(h * wide, wide)

    def source(c, rows):
        m, h, kv = CHUNKS[c]
        return sources[kv].at[m, rows, half(h)]

    def spot(c, rows):
        m, h, kv = CHUNKS[c]
        return span.at[kv, m, rows, half(h)]

    def terms_at(ref, t, rows):
        h, kv = TERMS[t]
        return ref.at[kv, rows, half(h)]

    def loads(m, kv):
        return pltpu.make_async_copy(
            sources[kv].at[m], span.at[kv, m, pl.ds(WINDOW, ROWS)], loc_sem.at[m * 2 + kv]
        )

    @pl.when(me == 0)
    def _():
        span[:, :, 0:WINDOW, :] = jnp.zeros((2, 2, WINDOW, span.shape[3]), span.dtype)

    @pl.when(me == 1)
    def _():
        span[:, :, 0:ROWS, :] = jnp.zeros((2, 2, ROWS, span.shape[3]), span.dtype)

    @pl.when(me >= tops * 2 * COLUMNS - 2)
    def _():
        got[...] = jnp.zeros_like(got)

    for m in (1, 0):
        for kv in range(2):
            loads(m, kv).start()

    barrier = pltpu.get_barrier_semaphore()
    pl.semaphore_signal(barrier, inc=1, device_id=mate, device_id_type=MESH)
    pl.semaphore_signal(barrier, inc=1, device_id=after, device_id_type=MESH)
    pl.semaphore_signal(barrier, inc=1, device_id=before, device_id_type=MESH)
    for step in range(1, COLUMNS):
        pl.semaphore_signal(
            barrier,
            inc=1,
            device_id=at(top, lax.rem(y + step, COLUMNS)),
            device_id_type=MESH,
        )


    @pl.when(has_next)
    def _():
        pl.semaphore_signal(barrier, inc=1, device_id=at(top + 1, y), device_id_type=MESH)

    @pl.when(has_prev)
    def _():
        pl.semaphore_signal(barrier, inc=1, device_id=at(top - 1, y), device_id_type=MESH)

    column_of = lax.broadcasted_iota(jnp.int32, (ROWS, ROWS), 1)
    row_of = lax.broadcasted_iota(jnp.int32, (ROWS, ROWS), 0)
    for m in range(2):
        here = pl.ds(pl.multiple_of(me * ROWS, ROWS), ROWS)
        seg_query = jnp.broadcast_to(seg_ref[m : m + 1, here].astype(jnp.float32), (ROWS, ROWS))
        for part in range(3):
            block = jnp.maximum(me - 2 + part, 0)
            there = pl.ds(pl.multiple_of(block * ROWS, ROWS), ROWS)
            seg_key = jnp.broadcast_to(seg_ref[m : m + 1, there].astype(jnp.float32), (ROWS, ROWS)).T
            offset = column_of + WINDOW - part * ROWS - row_of
            allowed = (seg_query == seg_key) & (offset >= 0) & (offset < WINDOW)
            allowed = allowed & (row_of + (part - 2 + me) * ROWS >= 0)
            value = jnp.where(allowed, 0.0, masked_score)
            bias[m, part * ROWS : (part + 1) * ROWS, 0:ROWS] = value
            bias[m, part * ROWS : (part + 1) * ROWS, ROWS : 2 * ROWS] = value

    across = jnp.minimum(top, 1) + jnp.minimum(tops - 1 - top, 1)
    pl.semaphore_wait(barrier, 3 + COLUMNS - 1 + across)

    def halo_b(c, src):
        @pl.when(y == 0)
        def _():
            copy(src, spot(c, piece(0)), b_send.at[c], b_recv.at[c], at(top + 1, y)).start()

        @pl.when(y > 0)
        def _():
            copy(src, rel_b.at[c], b_send.at[c], b_recv.at[c], at(top + 1, y)).start()

    crossing = (y == last) & has_next
    for c in range(len(CHUNKS)):

        @pl.when(crossing)
        def _():
            for q in range(last):
                copy(
                    source(c, piece(q)), rel_a.at[c], a_send.at[c, q], a_recv.at[c], at(top, q)
                ).start()
            copy(
                source(c, piece(last)), rel_b.at[c], b_send.at[c], b_recv.at[c], at(top + 1, last)
            ).start()

        @pl.when(y < last)
        def _():
            copy(
                source(c, all_rows), spot(c, all_rows), r_send.at[c], r_recv.at[c], at(top, y + 1)
            ).start()

        @pl.when(core == 0)
        def _():
            copy(
                source(c, all_rows), spot(c, near_rows), e_send.at[c], e_recv.at[c], mate
            ).start()

    def relay_b(c):
        @pl.when((y < last) & has_next)
        def _():
            arrived(rel_a.at[c], a_recv.at[c])
            halo_b(c, rel_a.at[c])

    def relay_c(c):
        @pl.when((y > 0) & has_prev)
        def _():
            arrived(rel_b.at[c], b_recv.at[c])
            for q in range(1, COLUMNS):

                @pl.when(y == q)
                def _():
                    copy(
                        rel_b.at[c], spot(c, piece(q)), c_send.at[c], c_recv.at[c, q], at(top, 0)
                    ).start()

    def pass_on(c):
        @pl.when((y == 0) & has_prev)
        def _():
            arrived(spot(c, piece(0)), b_recv.at[c])
            for q in range(1, COLUMNS):
                arrived(spot(c, piece(q)), c_recv.at[c, q])

        @pl.when(y > 0)
        def _():
            arrived(spot(c, all_rows), r_recv.at[c])

        @pl.when((core == 1) & (me >= 2))
        def _():
            copy(
                spot(c, all_rows), spot(c, near_rows), e_send.at[c], e_recv.at[c], mate
            ).start()

    def span_ready(c):
        m, h, kv = CHUNKS[c]

        @pl.when(me > 0)
        def _():
            arrived(spot(c, near_rows), e_recv.at[c])

        if h == 0:
            loads(m, kv).wait()

    def pair_of(ref, index, g):
        first = pl.multiple_of(g * 2 * HEAD_DIM, HEAD_DIM)
        second = pl.multiple_of(g * 2 * HEAD_DIM + HEAD_DIM, HEAD_DIM)
        return jnp.concatenate(
            [
                ref[index + (slice(None), pl.ds(first, HEAD_DIM))],
                ref[index + (slice(None), pl.ds(second, HEAD_DIM))],
            ],
            axis=0,
        )

    def store_pair(ref, g, value):
        first = pl.multiple_of(g * 2 * HEAD_DIM, HEAD_DIM)
        second = pl.multiple_of(g * 2 * HEAD_DIM + HEAD_DIM, HEAD_DIM)
        ref[:, pl.ds(first, HEAD_DIM)] = value[:ROWS].astype(ref.dtype)
        ref[:, pl.ds(second, HEAD_DIM)] = value[ROWS:].astype(ref.dtype)

    def probs_of(m, g):
        columns = pl.ds(pl.multiple_of(g * HEAD_DIM, HEAD_DIM), HEAD_DIM)
        keys = span[0, m, :, columns]
        values = span[1, m, :, columns]
        queries = pair_of(q_ref, (m,), g)
        scores = last_last(keys, queries) * score_scale + bias[m]
        weights = jnp.exp(scores - jnp.max(scores, axis=0, keepdims=True))
        probs = weights * (1.0 / jnp.sum(weights, axis=0, keepdims=True))
        return keys, values, queries, probs

    def backward(g, carry):
        keys, values, queries, probs = probs_of(1, g)
        columns = pl.ds(pl.multiple_of(g * HEAD_DIM, HEAD_DIM), HEAD_DIM)
        grads = pair_of(do_ref, (), g)
        rounded = probs.astype(jnp.bfloat16)
        grad_probs = last_last(values, grads)
        delta = jnp.sum(probs * grad_probs, axis=0, keepdims=True)
        grad_scores = (probs * score_scale * (grad_probs - delta)).astype(jnp.bfloat16)
        store_pair(dq, g, first_first(grad_scores, keys))
        for kv, terms in enumerate(
            (
                jnp.dot(grad_scores, queries, preferred_element_type=jnp.float32),
                jnp.dot(rounded, grads, preferred_element_type=jnp.float32),
            )
        ):
            far[kv, :, columns] = terms[0:ROWS].astype(jnp.bfloat16)
            near[kv, :, columns] = terms[ROWS:WINDOW].astype(jnp.bfloat16)
            own[kv, :, columns] = terms[WINDOW:]
        return carry

    def forward(g, carry):
        _, values, _, probs = probs_of(0, g)
        store_pair(att, g, first_first(probs.astype(jnp.bfloat16), values))
        return carry

    q_wide = q_ref.shape[-1] // 2
    half_heads = kv_heads // 2

    def q_half(ref, h):
        return ref.at[:, pl.ds(h * q_wide, q_wide)]

    def send_near(h):
        for kv in range(2):
            t = h * 2 + kv
            copy(
                terms_at(near, t, all_rows),
                terms_at(mate_near, t, all_rows),
                f_send.at[t],
                f_recv.at[t],
                mate,
            ).start()

    def send_queries(h):
        copy(q_half(dq, h), q_half(dq_out, h), s_send.at[2 + h], s_recv.at[2 + h], before).start()

    def send_attended(h):
        copy(q_half(att, h), q_half(att_out, h), s_send.at[h], s_recv.at[h], after).start()

    back_crossing = (y == 0) & has_prev

    def send_far(t):
        h, kv = TERMS[t]
        arrived(terms_at(mate_near, t, all_rows), f_recv.at[t])

        @pl.when(core == 1)
        def _():
            lanes = slice(h * wide, (h + 1) * wide)
            far[kv, :, lanes] = (
                far[kv, :, lanes].astype(jnp.float32)
                + mate_near[kv, :, lanes].astype(jnp.float32)
            ).astype(jnp.bfloat16)

        @pl.when(y > 0)
        def _():
            copy(
                terms_at(far, t, all_rows),
                terms_at(got, t, all_rows),
                g_send.at[t],
                g_recv.at[t],
                at(top, y - 1),
            ).start()

        @pl.when(back_crossing)
        def _():
            for q in range(1, COLUMNS):
                copy(
                    terms_at(far, t, piece(q)),
                    back_a.at[t],
                    ba_send.at[t, q],
                    ba_recv.at[t],
                    at(top, q),
                ).start()
            copy(
                terms_at(far, t, piece(0)),
                back_b.at[t],
                bb_send.at[t],
                bb_recv.at[t],
                at(top - 1, 0),
            ).start()

    def relay_back_b(t):
        @pl.when((y > 0) & has_prev)
        def _():
            arrived(back_a.at[t], ba_recv.at[t])

            @pl.when(y == last)
            def _():
                copy(
                    back_a.at[t],
                    terms_at(got, t, piece(last)),
                    bb_send.at[t],
                    bb_recv.at[t],
                    at(top - 1, y),
                ).start()

            @pl.when(y < last)
            def _():
                copy(
                    back_a.at[t], back_b.at[t], bb_send.at[t], bb_recv.at[t], at(top - 1, y)
                ).start()

    def relay_back_c(t):
        @pl.when((y < last) & has_next)
        def _():
            arrived(back_b.at[t], bb_recv.at[t])
            for q in range(last):

                @pl.when(y == q)
                def _():
                    copy(
                        back_b.at[t],
                        terms_at(got, t, piece(q)),
                        bc_send.at[t],
                        bc_recv.at[t, q],
                        at(top, last),
                    ).start()

    outs = (dk_out, dv_out)

    def finish_near(t):
        @pl.when(y < last)
        def _():
            arrived(terms_at(got, t, all_rows), g_recv.at[t])
            finish(t)

    def finish_across(t):
        @pl.when(y == last)
        def _():
            @pl.when(has_next)
            def _():
                arrived(terms_at(got, t, piece(last)), bb_recv.at[t])
                for q in range(last):
                    arrived(terms_at(got, t, piece(q)), bc_recv.at[t, q])

            finish(t)

    def finish(t):
        h, kv = TERMS[t]
        lanes = slice(h * wide, (h + 1) * wide)
        total = own[kv, :, lanes] + got[kv, :, lanes].astype(jnp.float32)

        @pl.when(core == 0)
        def _():
            final[kv, :, lanes] = (total + mate_near[kv, :, lanes].astype(jnp.float32)).astype(
                jnp.bfloat16
            )

        @pl.when(core == 1)
        def _():
            final[kv, :, lanes] = total.astype(jnp.bfloat16)

        copy(
            terms_at(final, t, all_rows),
            outs[kv].at[:, half(h)],
            s_send.at[4 + t],
            s_recv.at[4 + t],
            before,
        ).start()

    for c in range(8):
        relay_b(c)
    for c in (0, 1):
        relay_c(c)
    for c in (0, 1):
        pass_on(c)
    for c in (0, 1):
        span_ready(c)
    lax.fori_loop(0, half_heads, backward, 0)
    send_near(0)
    send_queries(0)
    for c in (2, 3):
        relay_c(c)
    for c in (2, 3):
        pass_on(c)
    for t in (0, 1):
        send_far(t)
    for c in (2, 3):
        span_ready(c)
    lax.fori_loop(half_heads, kv_heads, backward, 0)
    send_near(1)
    send_queries(1)
    for t in (0, 1):
        relay_back_b(t)
    for t in (2, 3):
        send_far(t)
    for c in (4, 5):
        relay_c(c)
    for t in (2, 3):
        relay_back_b(t)
    for c in (6, 7):
        relay_c(c)
    for c in (4, 5):
        pass_on(c)
    for c in (4, 5):
        span_ready(c)
    lax.fori_loop(0, half_heads, forward, 0)
    send_attended(0)
    for t in (0, 1):
        finish_near(t)
    for t in (0, 1):
        relay_back_c(t)
    for c in (6, 7):
        pass_on(c)
    for c in (6, 7):
        span_ready(c)
    lax.fori_loop(half_heads, kv_heads, forward, 0)
    send_attended(1)
    for t in (2, 3):
        finish_near(t)
    for t in (2, 3):
        relay_back_c(t)
    for t in range(4):
        finish_across(t)

    for c in range(len(CHUNKS)):

        @pl.when(crossing)
        def _():
            for q in range(last):
                sent(source(c, piece(q)), a_send.at[c, q])

        @pl.when(has_next)
        def _():
            sent(rel_a.at[c], b_send.at[c])

        @pl.when(y < last)
        def _():
            sent(source(c, all_rows), r_send.at[c])

        @pl.when((y > 0) & has_prev)
        def _():
            sent(rel_b.at[c], c_send.at[c])

        @pl.when((core == 0) | (me >= 2))
        def _():
            sent(source(c, all_rows), e_send.at[c])

    for t in range(len(TERMS)):
        sent(terms_at(near, t, all_rows), f_send.at[t])

        @pl.when(y > 0)
        def _():
            sent(terms_at(far, t, all_rows), g_send.at[t])

        @pl.when(back_crossing)
        def _():
            for q in range(1, COLUMNS):
                sent(terms_at(far, t, piece(q)), ba_send.at[t, q])

        @pl.when(has_prev)
        def _():
            sent(back_a.at[t], bb_send.at[t])

        @pl.when((y < last) & has_next)
        def _():
            sent(back_b.at[t], bc_send.at[t])

    moved = [(q_half(att, h), q_half(att_out, h)) for h in range(2)]
    moved += [(q_half(dq, h), q_half(dq_out, h)) for h in range(2)]
    moved += [(terms_at(final, t, all_rows), outs[t % 2].at[:, half(t // 2)]) for t in range(4)]
    for i, (src, dst) in enumerate(moved):
        sent(src, s_send.at[i])
        arrived(dst, s_recv.at[i])


def shards(tops, sections, queries, keys, values, out_grad, segments):
    q_width = queries.shape[-1]
    k_width = keys.shape[-1]
    kv_heads = k_width // HEAD_DIM
    half, full = jnp.bfloat16, jnp.float32
    vmem = pl.BlockSpec(memory_space=pltpu.VMEM)
    hbm = pl.BlockSpec(memory_space=pl.ANY)
    dma = pltpu.SemaphoreType.DMA
    results = pl.pallas_call(
        functools.partial(kernel, tops, sections, kv_heads),
        out_shape=[
            jax.ShapeDtypeStruct((ROWS, q_width), half),
            jax.ShapeDtypeStruct((ROWS, q_width), half),
            jax.ShapeDtypeStruct((ROWS, k_width), half),
            jax.ShapeDtypeStruct((ROWS, k_width), half),
        ],
        in_specs=[vmem, hbm, hbm, vmem, vmem],
        out_specs=[hbm] * 4,
        scratch_shapes=[
            pltpu.VMEM((2, 2, WINDOW + ROWS, k_width), half),
            pltpu.VMEM((2, WINDOW + ROWS, 2 * ROWS), full),
            pltpu.VMEM((ROWS, q_width), half),
            pltpu.VMEM((ROWS, q_width), half),
            pltpu.VMEM((2, ROWS, k_width), half),
            pltpu.VMEM((2, ROWS, k_width), half),
            pltpu.VMEM((2, ROWS, k_width), full),
            pltpu.VMEM((2, ROWS, k_width), half),
            pltpu.VMEM((2, ROWS, k_width), half),
            pltpu.VMEM((2, ROWS, k_width), half),
            pltpu.VMEM((8, PIECE, k_width // 2), half),
            pltpu.VMEM((8, PIECE, k_width // 2), half),
            pltpu.VMEM((4, PIECE, k_width // 2), half),
            pltpu.VMEM((4, PIECE, k_width // 2), half),
            dma((4,)),
            dma((8,)),
            dma((8,)),
            dma((8, COLUMNS)),
            dma((8,)),
            dma((8,)),
            dma((8,)),
            dma((8,)),
            dma((8, COLUMNS)),
            dma((8,)),
            dma((8,)),
            dma((4,)),
            dma((4,)),
            dma((4,)),
            dma((4,)),
            dma((4, COLUMNS)),
            dma((4,)),
            dma((4,)),
            dma((4,)),
            dma((4,)),
            dma((4, COLUMNS)),
            dma((8,)),
            dma((8,)),
        ],
        compiler_params=pltpu.CompilerParams(collective_id=0, has_side_effects=True),
    )(queries[0], keys[0], values[0], out_grad[0], segments)
    return tuple(result[None] for result in results)


def solution(mesh):
    tops = mesh.shape["seq"] // (2 * COLUMNS)
    sections = mesh.shape["section"]
    return jax.shard_map(
        functools.partial(shards, tops, sections),
        mesh=mesh,
        in_specs=(
            P("section", None, "seq", None),
            P("section", None, "seq", None),
            P("section", None, "seq", None),
            P("section", "seq", None),
            P(),
        ),
        out_specs=(
            P("section", "seq", None),
            P("section", "seq", None),
            P("section", "seq", None),
            P("section", "seq", None),
        ),
        check_vma=False,
    )
```

```python
import functools

import jax
import jax.numpy as jnp
from jax import lax
from jax.experimental import pallas as pl
from jax.experimental.pallas import tpu as pltpu
from jax.sharding import PartitionSpec as P

HEAD_DIM = 128
WINDOW = 256
ROWS = 128
COLUMNS = 4
SECTION_RUN = 4
PIECE = ROWS // COLUMNS
MESH = pl.DeviceIdType.MESH

score_scale = 168.0 ** (-0.5)
masked_score = -1e30

CHUNKS = tuple((m, h, kv) for m in (1, 0) for h in range(2) for kv in range(2))
TERMS = tuple((h, kv) for h in range(2) for kv in range(2))


def last_last(a, b):
    return lax.dot_general(a, b, (((1,), (1,)), ((), ())), preferred_element_type=jnp.float32)


def first_first(a, b):
    return lax.dot_general(a, b, (((0,), (0,)), ((), ())), preferred_element_type=jnp.float32)


def kernel(
    tops,
    sections,
    kv_heads,
    q_ref,
    k_ref,
    v_ref,
    do_ref,
    seg_ref,
    att_out,
    dq_out,
    dk_out,
    dv_out,
    span,
    bias,
    att,
    dq,
    near,
    far,
    own,
    mate_near,
    got,
    final,
    rel_a,
    rel_b,
    back_a,
    back_b,
    loc_sem,
    r_send,
    r_recv,
    a_send,
    a_recv,
    b_send,
    b_recv,
    c_send,
    c_recv,
    e_send,
    e_recv,
    f_send,
    f_recv,
    g_send,
    g_recv,
    ba_send,
    ba_recv,
    bb_send,
    bb_recv,
    bc_send,
    bc_recv,
    s_send,
    s_recv,
):
    me = lax.axis_index("seq")
    sec = lax.axis_index("section")
    core = lax.rem(me, 2)
    y = lax.rem(lax.div(me, 2), COLUMNS)
    top = lax.div(me, 2 * COLUMNS)
    last = COLUMNS - 1

    def at(top_of, y_of):
        return ((top_of * COLUMNS + y_of) * 2 + core, sec)

    mate = (me + 1 - 2 * core, sec)
    after = (me, lax.rem(sec + 1, sections))
    before = (me, lax.rem(sec + sections - 1, sections))
    yields_back = (lax.rem(sec, SECTION_RUN) == 0) & (sec > 0) & (y < last)
    yields_on = sec == sections - 1
    has_next = top < tops - 1
    has_prev = top > 0

    def copy(src, dst, send, recv, device):
        return pltpu.make_async_remote_copy(
            src_ref=src,
            dst_ref=dst,
            send_sem=send,
            recv_sem=recv,
            device_id=device,
            device_id_type=MESH,
        )

    def arrived(dst, recv):
        copy(dst, dst, e_send.at[0], recv, mate).wait_recv()

    def sent(src, send):
        copy(src, src, send, e_recv.at[0], mate).wait_send()

    sources = (k_ref, v_ref)
    wide = k_ref.shape[-1] // 2
    all_rows = pl.ds(0, ROWS)
    near_rows = pl.ds(ROWS, ROWS)

    def piece(q):
        return pl.ds(q * PIECE, PIECE)

    def half(h):
        return pl.ds(h * wide, wide)

    def source(c, rows):
        m, h, kv = CHUNKS[c]
        return sources[kv].at[m, rows, half(h)]

    def spot(c, rows):
        m, h, kv = CHUNKS[c]
        return span.at[kv, m, rows, half(h)]

    def terms_at(ref, t, rows):
        h, kv = TERMS[t]
        return ref.at[kv, rows, half(h)]

    def loads(m, kv):
        return pltpu.make_async_copy(
            sources[kv].at[m], span.at[kv, m, pl.ds(WINDOW, ROWS)], loc_sem.at[m * 2 + kv]
        )

    @pl.when(me == 0)
    def _():
        span[:, :, 0:WINDOW, :] = jnp.zeros((2, 2, WINDOW, span.shape[3]), span.dtype)

    @pl.when(me == 1)
    def _():
        span[:, :, 0:ROWS, :] = jnp.zeros((2, 2, ROWS, span.shape[3]), span.dtype)

    @pl.when(me >= tops * 2 * COLUMNS - 2)
    def _():
        got[...] = jnp.zeros_like(got)

    for m in (1, 0):
        for kv in range(2):
            loads(m, kv).start()

    barrier = pltpu.get_barrier_semaphore()
    pl.semaphore_signal(barrier, inc=1, device_id=mate, device_id_type=MESH)
    pl.semaphore_signal(barrier, inc=1, device_id=after, device_id_type=MESH)
    pl.semaphore_signal(barrier, inc=1, device_id=before, device_id_type=MESH)
    for step in range(1, COLUMNS):
        pl.semaphore_signal(
            barrier,
            inc=1,
            device_id=at(top, lax.rem(y + step, COLUMNS)),
            device_id_type=MESH,
        )


    @pl.when(has_next)
    def _():
        pl.semaphore_signal(barrier, inc=1, device_id=at(top + 1, y), device_id_type=MESH)

    @pl.when(has_prev)
    def _():
        pl.semaphore_signal(barrier, inc=1, device_id=at(top - 1, y), device_id_type=MESH)

    column_of = lax.broadcasted_iota(jnp.int32, (ROWS, ROWS), 1)
    row_of = lax.broadcasted_iota(jnp.int32, (ROWS, ROWS), 0)
    for m in range(2):
        here = pl.ds(pl.multiple_of(me * ROWS, ROWS), ROWS)
        seg_query = jnp.broadcast_to(seg_ref[m : m + 1, here].astype(jnp.float32), (ROWS, ROWS))
        for part in range(3):
            block = jnp.maximum(me - 2 + part, 0)
            there = pl.ds(pl.multiple_of(block * ROWS, ROWS), ROWS)
            seg_key = jnp.broadcast_to(seg_ref[m : m + 1, there].astype(jnp.float32), (ROWS, ROWS)).T
            offset = column_of + WINDOW - part * ROWS - row_of
            allowed = (seg_query == seg_key) & (offset >= 0) & (offset < WINDOW)
            allowed = allowed & (row_of + (part - 2 + me) * ROWS >= 0)
            value = jnp.where(allowed, 0.0, masked_score)
            bias[m, part * ROWS : (part + 1) * ROWS, 0:ROWS] = value
            bias[m, part * ROWS : (part + 1) * ROWS, ROWS : 2 * ROWS] = value

    across = jnp.minimum(top, 1) + jnp.minimum(tops - 1 - top, 1)
    pl.semaphore_wait(barrier, 3 + COLUMNS - 1 + across)

    def halo_b(c, src):
        @pl.when(y == 0)
        def _():
            copy(src, spot(c, piece(0)), b_send.at[c], b_recv.at[c], at(top + 1, y)).start()

        @pl.when(y > 0)
        def _():
            copy(src, rel_b.at[c], b_send.at[c], b_recv.at[c], at(top + 1, y)).start()

    crossing = (y == last) & has_next
    for c in range(len(CHUNKS)):

        @pl.when(crossing)
        def _():
            for q in range(last):
                copy(
                    source(c, piece(q)), rel_a.at[c], a_send.at[c, q], a_recv.at[c], at(top, q)
                ).start()
            copy(
                source(c, piece(last)), rel_b.at[c], b_send.at[c], b_recv.at[c], at(top + 1, last)
            ).start()

        @pl.when(y < last)
        def _():
            copy(
                source(c, all_rows), spot(c, all_rows), r_send.at[c], r_recv.at[c], at(top, y + 1)
            ).start()

        @pl.when(core == 0)
        def _():
            copy(
                source(c, all_rows), spot(c, near_rows), e_send.at[c], e_recv.at[c], mate
            ).start()

    def relay_b(c):
        @pl.when((y < last) & has_next)
        def _():
            arrived(rel_a.at[c], a_recv.at[c])
            halo_b(c, rel_a.at[c])

    def relay_c(c):
        @pl.when((y > 0) & has_prev)
        def _():
            arrived(rel_b.at[c], b_recv.at[c])
            for q in range(1, COLUMNS):

                @pl.when(y == q)
                def _():
                    copy(
                        rel_b.at[c], spot(c, piece(q)), c_send.at[c], c_recv.at[c, q], at(top, 0)
                    ).start()

    def pass_on(c):
        @pl.when((y == 0) & has_prev)
        def _():
            arrived(spot(c, piece(0)), b_recv.at[c])
            for q in range(1, COLUMNS):
                arrived(spot(c, piece(q)), c_recv.at[c, q])

        @pl.when(y > 0)
        def _():
            arrived(spot(c, all_rows), r_recv.at[c])

        @pl.when((core == 1) & (me >= 2))
        def _():
            copy(
                spot(c, all_rows), spot(c, near_rows), e_send.at[c], e_recv.at[c], mate
            ).start()

    def span_ready(c):
        m, h, kv = CHUNKS[c]

        @pl.when(me > 0)
        def _():
            arrived(spot(c, near_rows), e_recv.at[c])

        if h == 0:
            loads(m, kv).wait()

    def pair_of(ref, index, g):
        first = pl.multiple_of(g * 2 * HEAD_DIM, HEAD_DIM)
        second = pl.multiple_of(g * 2 * HEAD_DIM + HEAD_DIM, HEAD_DIM)
        return jnp.concatenate(
            [
                ref[index + (slice(None), pl.ds(first, HEAD_DIM))],
                ref[index + (slice(None), pl.ds(second, HEAD_DIM))],
            ],
            axis=0,
        )

    def store_pair(ref, g, value):
        first = pl.multiple_of(g * 2 * HEAD_DIM, HEAD_DIM)
        second = pl.multiple_of(g * 2 * HEAD_DIM + HEAD_DIM, HEAD_DIM)
        ref[:, pl.ds(first, HEAD_DIM)] = value[:ROWS].astype(ref.dtype)
        ref[:, pl.ds(second, HEAD_DIM)] = value[ROWS:].astype(ref.dtype)

    def probs_of(m, g):
        columns = pl.ds(pl.multiple_of(g * HEAD_DIM, HEAD_DIM), HEAD_DIM)
        keys = span[0, m, :, columns]
        values = span[1, m, :, columns]
        queries = pair_of(q_ref, (m,), g)
        scores = last_last(keys, queries) * score_scale + bias[m]
        weights = jnp.exp(scores - jnp.max(scores, axis=0, keepdims=True))
        probs = weights * (1.0 / jnp.sum(weights, axis=0, keepdims=True))
        return keys, values, queries, probs

    def backward(g, carry):
        keys, values, queries, probs = probs_of(1, g)
        columns = pl.ds(pl.multiple_of(g * HEAD_DIM, HEAD_DIM), HEAD_DIM)
        grads = pair_of(do_ref, (), g)
        rounded = probs.astype(jnp.bfloat16)
        grad_probs = last_last(values, grads)
        delta = jnp.sum(probs * grad_probs, axis=0, keepdims=True)
        grad_scores = (probs * score_scale * (grad_probs - delta)).astype(jnp.bfloat16)
        store_pair(dq, g, first_first(grad_scores, keys))
        for kv, terms in enumerate(
            (
                jnp.dot(grad_scores, queries, preferred_element_type=jnp.float32),
                jnp.dot(rounded, grads, preferred_element_type=jnp.float32),
            )
        ):
            far[kv, :, columns] = terms[0:ROWS].astype(jnp.bfloat16)
            near[kv, :, columns] = terms[ROWS:WINDOW].astype(jnp.bfloat16)
            own[kv, :, columns] = terms[WINDOW:]
        return carry

    def forward(g, carry):
        _, values, _, probs = probs_of(0, g)
        store_pair(att, g, first_first(probs.astype(jnp.bfloat16), values))
        return carry

    q_wide = q_ref.shape[-1] // 2
    half_heads = kv_heads // 2

    def q_half(ref, h):
        return ref.at[:, pl.ds(h * q_wide, q_wide)]

    def send_near(h):
        for kv in range(2):
            t = h * 2 + kv
            copy(
                terms_at(near, t, all_rows),
                terms_at(mate_near, t, all_rows),
                f_send.at[t],
                f_recv.at[t],
                mate,
            ).start()

    def send_queries(h):
        copy(q_half(dq, h), q_half(dq_out, h), s_send.at[2 + h], s_recv.at[2 + h], before).start()

    def send_attended(h):
        copy(q_half(att, h), q_half(att_out, h), s_send.at[h], s_recv.at[h], after).start()

    back_crossing = (y == 0) & has_prev

    def send_far(t):
        h, kv = TERMS[t]
        arrived(terms_at(mate_near, t, all_rows), f_recv.at[t])

        @pl.when(core == 1)
        def _():
            lanes = slice(h * wide, (h + 1) * wide)
            far[kv, :, lanes] = (
                far[kv, :, lanes].astype(jnp.float32)
                + mate_near[kv, :, lanes].astype(jnp.float32)
            ).astype(jnp.bfloat16)

        @pl.when(y > 0)
        def _():
            copy(
                terms_at(far, t, all_rows),
                terms_at(got, t, all_rows),
                g_send.at[t],
                g_recv.at[t],
                at(top, y - 1),
            ).start()

        @pl.when(back_crossing)
        def _():
            for q in range(1, COLUMNS):
                copy(
                    terms_at(far, t, piece(q)),
                    back_a.at[t],
                    ba_send.at[t, q],
                    ba_recv.at[t],
                    at(top, q),
                ).start()
            copy(
                terms_at(far, t, piece(0)),
                back_b.at[t],
                bb_send.at[t],
                bb_recv.at[t],
                at(top - 1, 0),
            ).start()

    def relay_back_b(t):
        @pl.when((y > 0) & has_prev)
        def _():
            arrived(back_a.at[t], ba_recv.at[t])

            @pl.when(y == last)
            def _():
                copy(
                    back_a.at[t],
                    terms_at(got, t, piece(last)),
                    bb_send.at[t],
                    bb_recv.at[t],
                    at(top - 1, y),
                ).start()

            @pl.when(y < last)
            def _():
                copy(
                    back_a.at[t], back_b.at[t], bb_send.at[t], bb_recv.at[t], at(top - 1, y)
                ).start()

    def relay_back_c(t):
        @pl.when((y < last) & has_next)
        def _():
            arrived(back_b.at[t], bb_recv.at[t])
            for q in range(last):

                @pl.when(y == q)
                def _():
                    copy(
                        back_b.at[t],
                        terms_at(got, t, piece(q)),
                        bc_send.at[t],
                        bc_recv.at[t, q],
                        at(top, last),
                    ).start()

    outs = (dk_out, dv_out)

    def finish_near(t):
        @pl.when(y < last)
        def _():
            arrived(terms_at(got, t, all_rows), g_recv.at[t])
            finish(t)

    def finish_across(t):
        @pl.when(y == last)
        def _():
            @pl.when(has_next)
            def _():
                arrived(terms_at(got, t, piece(last)), bb_recv.at[t])
                for q in range(last):
                    arrived(terms_at(got, t, piece(q)), bc_recv.at[t, q])

            finish(t)

    def finish(t):
        h, kv = TERMS[t]
        lanes = slice(h * wide, (h + 1) * wide)
        total = own[kv, :, lanes] + got[kv, :, lanes].astype(jnp.float32)

        @pl.when(core == 0)
        def _():
            final[kv, :, lanes] = (total + mate_near[kv, :, lanes].astype(jnp.float32)).astype(
                jnp.bfloat16
            )

        @pl.when(core == 1)
        def _():
            final[kv, :, lanes] = total.astype(jnp.bfloat16)

        @pl.when(jnp.logical_not(yields_back))
        def _():
            send_terms(t)

    def send_terms(t):
        h, kv = TERMS[t]
        copy(
            terms_at(final, t, all_rows),
            outs[kv].at[:, half(h)],
            s_send.at[4 + t],
            s_recv.at[4 + t],
            before,
        ).start()

    for c in range(8):
        relay_b(c)
    for c in (0, 1):
        relay_c(c)
    for c in (0, 1):
        pass_on(c)
    for c in (0, 1):
        span_ready(c)
    lax.fori_loop(0, half_heads, backward, 0)
    send_near(0)
    send_queries(0)
    for c in (2, 3):
        relay_c(c)
    for c in (2, 3):
        pass_on(c)
    for t in (0, 1):
        send_far(t)
    for c in (2, 3):
        span_ready(c)
    lax.fori_loop(half_heads, kv_heads, backward, 0)
    send_near(1)

    @pl.when(jnp.logical_not(yields_back))
    def _():
        send_queries(1)

    for t in (0, 1):
        relay_back_b(t)
    for t in (2, 3):
        send_far(t)
    for c in (4, 5):
        relay_c(c)
    for t in (2, 3):
        relay_back_b(t)
    for c in (6, 7):
        relay_c(c)
    for c in (4, 5):
        pass_on(c)
    for c in (4, 5):
        span_ready(c)
    lax.fori_loop(0, half_heads, forward, 0)

    @pl.when(jnp.logical_not(yields_on))
    def _():
        send_attended(0)

    for t in (0, 1):
        finish_near(t)
    for t in (0, 1):
        relay_back_c(t)
    for c in (6, 7):
        pass_on(c)
    for c in (6, 7):
        span_ready(c)
    lax.fori_loop(half_heads, kv_heads, forward, 0)

    @pl.when(jnp.logical_not(yields_on))
    def _():
        send_attended(1)

    for t in (2, 3):
        finish_near(t)
    for t in (2, 3):
        relay_back_c(t)

    @pl.when(yields_back)
    def _():
        send_queries(1)
        for t in range(4):
            send_terms(t)

    @pl.when(yields_on)
    def _():
        for h in range(2):
            send_attended(h)

    for t in range(4):
        finish_across(t)

    for c in range(len(CHUNKS)):

        @pl.when(crossing)
        def _():
            for q in range(last):
                sent(source(c, piece(q)), a_send.at[c, q])

        @pl.when(has_next)
        def _():
            sent(rel_a.at[c], b_send.at[c])

        @pl.when(y < last)
        def _():
            sent(source(c, all_rows), r_send.at[c])

        @pl.when((y > 0) & has_prev)
        def _():
            sent(rel_b.at[c], c_send.at[c])

        @pl.when((core == 0) | (me >= 2))
        def _():
            sent(source(c, all_rows), e_send.at[c])

    for t in range(len(TERMS)):
        sent(terms_at(near, t, all_rows), f_send.at[t])

        @pl.when(y > 0)
        def _():
            sent(terms_at(far, t, all_rows), g_send.at[t])

        @pl.when(back_crossing)
        def _():
            for q in range(1, COLUMNS):
                sent(terms_at(far, t, piece(q)), ba_send.at[t, q])

        @pl.when(has_prev)
        def _():
            sent(back_a.at[t], bb_send.at[t])

        @pl.when((y < last) & has_next)
        def _():
            sent(back_b.at[t], bc_send.at[t])

    moved = [(q_half(att, h), q_half(att_out, h)) for h in range(2)]
    moved += [(q_half(dq, h), q_half(dq_out, h)) for h in range(2)]
    moved += [(terms_at(final, t, all_rows), outs[t % 2].at[:, half(t // 2)]) for t in range(4)]
    for i, (src, dst) in enumerate(moved):
        sent(src, s_send.at[i])
        arrived(dst, s_recv.at[i])


def shards(tops, sections, queries, keys, values, out_grad, segments):
    q_width = queries.shape[-1]
    k_width = keys.shape[-1]
    kv_heads = k_width // HEAD_DIM
    half, full = jnp.bfloat16, jnp.float32
    vmem = pl.BlockSpec(memory_space=pltpu.VMEM)
    hbm = pl.BlockSpec(memory_space=pl.ANY)
    dma = pltpu.SemaphoreType.DMA
    results = pl.pallas_call(
        functools.partial(kernel, tops, sections, kv_heads),
        out_shape=[
            pltpu.VMEM((ROWS, q_width), half),
            pltpu.VMEM((ROWS, q_width), half),
            pltpu.VMEM((ROWS, k_width), half),
            pltpu.VMEM((ROWS, k_width), half),
        ],
        in_specs=[vmem, hbm, hbm, vmem, vmem],
        out_specs=[hbm] * 4,
        scratch_shapes=[
            pltpu.VMEM((2, 2, WINDOW + ROWS, k_width), half),
            pltpu.VMEM((2, WINDOW + ROWS, 2 * ROWS), full),
            pltpu.VMEM((ROWS, q_width), half),
            pltpu.VMEM((ROWS, q_width), half),
            pltpu.VMEM((2, ROWS, k_width), half),
            pltpu.VMEM((2, ROWS, k_width), half),
            pltpu.VMEM((2, ROWS, k_width), full),
            pltpu.VMEM((2, ROWS, k_width), half),
            pltpu.VMEM((2, ROWS, k_width), half),
            pltpu.VMEM((2, ROWS, k_width), half),
            pltpu.VMEM((8, PIECE, k_width // 2), half),
            pltpu.VMEM((8, PIECE, k_width // 2), half),
            pltpu.VMEM((4, PIECE, k_width // 2), half),
            pltpu.VMEM((4, PIECE, k_width // 2), half),
            dma((4,)),
            dma((8,)),
            dma((8,)),
            dma((8, COLUMNS)),
            dma((8,)),
            dma((8,)),
            dma((8,)),
            dma((8,)),
            dma((8, COLUMNS)),
            dma((8,)),
            dma((8,)),
            dma((4,)),
            dma((4,)),
            dma((4,)),
            dma((4,)),
            dma((4, COLUMNS)),
            dma((4,)),
            dma((4,)),
            dma((4,)),
            dma((4,)),
            dma((4, COLUMNS)),
            dma((8,)),
            dma((8,)),
        ],
        compiler_params=pltpu.CompilerParams(collective_id=0, has_side_effects=True),
    )(queries[0], keys[0], values[0], out_grad[0], segments)
    return tuple(result[None] for result in results)


def solution(mesh):
    tops = mesh.shape["seq"] // (2 * COLUMNS)
    sections = mesh.shape["section"]
    return jax.shard_map(
        functools.partial(shards, tops, sections),
        mesh=mesh,
        in_specs=(
            P("section", None, "seq", None),
            P("section", None, "seq", None),
            P("section", None, "seq", None),
            P("section", "seq", None),
            P(),
        ),
        out_specs=(
            P("section", "seq", None),
            P("section", "seq", None),
            P("section", "seq", None),
            P("section", "seq", None),
        ),
        check_vma=False,
    )
```

```python
import functools

import jax
import jax.numpy as jnp
from jax import lax
from jax.experimental import pallas as pl
from jax.experimental.pallas import tpu as pltpu
from jax.sharding import PartitionSpec as P

HEAD_DIM = 128
WINDOW = 256
ROWS = 128
COLUMNS = 4
RUN = 4
PIECE = ROWS // COLUMNS
MESH = pl.DeviceIdType.MESH

score_scale = 168.0 ** (-0.5)
masked_score = -1e30

CHUNKS = tuple((m, h, kv) for m in (1, 0) for h in range(2) for kv in range(2))
TERMS = tuple((h, kv) for h in range(2) for kv in range(2))


def last_last(a, b):
    return lax.dot_general(a, b, (((1,), (1,)), ((), ())), preferred_element_type=jnp.float32)


def first_first(a, b):
    return lax.dot_general(a, b, (((0,), (0,)), ((), ())), preferred_element_type=jnp.float32)


def kernel(
    tops,
    sections,
    kv_heads,
    q_ref,
    k_ref,
    v_ref,
    do_ref,
    seg_ref,
    att_out,
    dq_out,
    dk_out,
    dv_out,
    span,
    bias,
    att,
    dq,
    near,
    far,
    own,
    mate_near,
    got,
    final,
    rel_a,
    rel_b,
    back_a,
    back_b,
    loc_sem,
    r_send,
    r_recv,
    a_send,
    a_recv,
    b_send,
    b_recv,
    c_send,
    c_recv,
    e_send,
    e_recv,
    f_send,
    f_recv,
    g_send,
    g_recv,
    ba_send,
    ba_recv,
    bb_send,
    bb_recv,
    bc_send,
    bc_recv,
    s_send,
    s_recv,
    turned,
    t_send,
    t_recv,
):
    me = lax.axis_index("seq")
    sec = lax.axis_index("section")
    core = lax.rem(me, 2)
    y = lax.rem(lax.div(me, 2), COLUMNS)
    top = lax.div(me, 2 * COLUMNS)
    last = COLUMNS - 1

    def at(top_of, y_of):
        return ((top_of * COLUMNS + y_of) * 2 + core, sec)

    mate = (me + 1 - 2 * core, sec)
    after = (me, lax.rem(sec + 1, sections))
    before = (me, lax.rem(sec + sections - 1, sections))
    x = lax.rem(sec, RUN)
    low = lax.div(sec, RUN)
    lows = sections // RUN
    turns = (x == 0) & (low > 0)
    corner = (x == RUN - 1) & (low > 0)
    corner_after = (x == RUN - 1) & (low < lows - 1)
    has_next = top < tops - 1
    has_prev = top > 0

    def copy(src, dst, send, recv, device):
        return pltpu.make_async_remote_copy(
            src_ref=src,
            dst_ref=dst,
            send_sem=send,
            recv_sem=recv,
            device_id=device,
            device_id_type=MESH,
        )

    def arrived(dst, recv):
        copy(dst, dst, e_send.at[0], recv, mate).wait_recv()

    def sent(src, send):
        copy(src, src, send, e_recv.at[0], mate).wait_send()

    sources = (k_ref, v_ref)
    wide = k_ref.shape[-1] // 2
    all_rows = pl.ds(0, ROWS)
    near_rows = pl.ds(ROWS, ROWS)

    def piece(q):
        return pl.ds(q * PIECE, PIECE)

    def half(h):
        return pl.ds(h * wide, wide)

    def source(c, rows):
        m, h, kv = CHUNKS[c]
        return sources[kv].at[m, rows, half(h)]

    def spot(c, rows):
        m, h, kv = CHUNKS[c]
        return span.at[kv, m, rows, half(h)]

    def terms_at(ref, t, rows):
        h, kv = TERMS[t]
        return ref.at[kv, rows, half(h)]

    def loads(m, kv):
        return pltpu.make_async_copy(
            sources[kv].at[m], span.at[kv, m, pl.ds(WINDOW, ROWS)], loc_sem.at[m * 2 + kv]
        )

    @pl.when(me == 0)
    def _():
        span[:, :, 0:WINDOW, :] = jnp.zeros((2, 2, WINDOW, span.shape[3]), span.dtype)

    @pl.when(me == 1)
    def _():
        span[:, :, 0:ROWS, :] = jnp.zeros((2, 2, ROWS, span.shape[3]), span.dtype)

    @pl.when(me >= tops * 2 * COLUMNS - 2)
    def _():
        got[...] = jnp.zeros_like(got)

    for m in (1, 0):
        for kv in range(2):
            loads(m, kv).start()

    barrier = pltpu.get_barrier_semaphore()
    pl.semaphore_signal(barrier, inc=1, device_id=mate, device_id_type=MESH)
    pl.semaphore_signal(barrier, inc=1, device_id=after, device_id_type=MESH)
    pl.semaphore_signal(barrier, inc=1, device_id=before, device_id_type=MESH)
    for step in range(1, COLUMNS):
        pl.semaphore_signal(
            barrier,
            inc=1,
            device_id=at(top, lax.rem(y + step, COLUMNS)),
            device_id_type=MESH,
        )


    @pl.when(has_next)
    def _():
        pl.semaphore_signal(barrier, inc=1, device_id=at(top + 1, y), device_id_type=MESH)

    @pl.when(has_prev)
    def _():
        pl.semaphore_signal(barrier, inc=1, device_id=at(top - 1, y), device_id_type=MESH)

    def greet(condition, section):
        @pl.when(condition)
        def _():
            pl.semaphore_signal(barrier, inc=1, device_id=(me, section), device_id_type=MESH)

    greet(turns, sec + RUN - 1)
    greet(corner, sec - RUN + 1)
    greet(corner, sec - RUN)
    greet(corner_after, sec + RUN)

    column_of = lax.broadcasted_iota(jnp.int32, (ROWS, ROWS), 1)
    row_of = lax.broadcasted_iota(jnp.int32, (ROWS, ROWS), 0)
    for m in range(2):
        here = pl.ds(pl.multiple_of(me * ROWS, ROWS), ROWS)
        seg_query = jnp.broadcast_to(seg_ref[m : m + 1, here].astype(jnp.float32), (ROWS, ROWS))
        for part in range(3):
            block = jnp.maximum(me - 2 + part, 0)
            there = pl.ds(pl.multiple_of(block * ROWS, ROWS), ROWS)
            seg_key = jnp.broadcast_to(seg_ref[m : m + 1, there].astype(jnp.float32), (ROWS, ROWS)).T
            offset = column_of + WINDOW - part * ROWS - row_of
            allowed = (seg_query == seg_key) & (offset >= 0) & (offset < WINDOW)
            allowed = allowed & (row_of + (part - 2 + me) * ROWS >= 0)
            value = jnp.where(allowed, 0.0, masked_score)
            bias[m, part * ROWS : (part + 1) * ROWS, 0:ROWS] = value
            bias[m, part * ROWS : (part + 1) * ROWS, ROWS : 2 * ROWS] = value

    across = jnp.minimum(top, 1) + jnp.minimum(tops - 1 - top, 1)
    first, final_x = 1 - jnp.minimum(x, 1), jnp.maximum(x - (RUN - 2), 0)
    behind, ahead = jnp.minimum(low, 1), jnp.minimum(lows - 1 - low, 1)
    turning = first * behind + final_x * (2 * behind + ahead)
    pl.semaphore_wait(barrier, 3 + COLUMNS - 1 + across + turning)

    def halo_b(c, src):
        @pl.when(y == 0)
        def _():
            copy(src, spot(c, piece(0)), b_send.at[c], b_recv.at[c], at(top + 1, y)).start()

        @pl.when(y > 0)
        def _():
            copy(src, rel_b.at[c], b_send.at[c], b_recv.at[c], at(top + 1, y)).start()

    crossing = (y == last) & has_next
    for c in range(len(CHUNKS)):

        @pl.when(crossing)
        def _():
            for q in range(last):
                copy(
                    source(c, piece(q)), rel_a.at[c], a_send.at[c, q], a_recv.at[c], at(top, q)
                ).start()
            copy(
                source(c, piece(last)), rel_b.at[c], b_send.at[c], b_recv.at[c], at(top + 1, last)
            ).start()

        @pl.when(y < last)
        def _():
            copy(
                source(c, all_rows), spot(c, all_rows), r_send.at[c], r_recv.at[c], at(top, y + 1)
            ).start()

        @pl.when(core == 0)
        def _():
            copy(
                source(c, all_rows), spot(c, near_rows), e_send.at[c], e_recv.at[c], mate
            ).start()

    def relay_b(c):
        @pl.when((y < last) & has_next)
        def _():
            arrived(rel_a.at[c], a_recv.at[c])
            halo_b(c, rel_a.at[c])

    def relay_c(c):
        @pl.when((y > 0) & has_prev)
        def _():
            arrived(rel_b.at[c], b_recv.at[c])
            for q in range(1, COLUMNS):

                @pl.when(y == q)
                def _():
                    copy(
                        rel_b.at[c], spot(c, piece(q)), c_send.at[c], c_recv.at[c, q], at(top, 0)
                    ).start()

    def pass_on(c):
        @pl.when((y == 0) & has_prev)
        def _():
            arrived(spot(c, piece(0)), b_recv.at[c])
            for q in range(1, COLUMNS):
                arrived(spot(c, piece(q)), c_recv.at[c, q])

        @pl.when(y > 0)
        def _():
            arrived(spot(c, all_rows), r_recv.at[c])

        @pl.when((core == 1) & (me >= 2))
        def _():
            copy(
                spot(c, all_rows), spot(c, near_rows), e_send.at[c], e_recv.at[c], mate
            ).start()

    def span_ready(c):
        m, h, kv = CHUNKS[c]

        @pl.when(me > 0)
        def _():
            arrived(spot(c, near_rows), e_recv.at[c])

        if h == 0:
            loads(m, kv).wait()

    def pair_of(ref, index, g):
        first = pl.multiple_of(g * 2 * HEAD_DIM, HEAD_DIM)
        second = pl.multiple_of(g * 2 * HEAD_DIM + HEAD_DIM, HEAD_DIM)
        return jnp.concatenate(
            [
                ref[index + (slice(None), pl.ds(first, HEAD_DIM))],
                ref[index + (slice(None), pl.ds(second, HEAD_DIM))],
            ],
            axis=0,
        )

    def store_pair(ref, g, value):
        first = pl.multiple_of(g * 2 * HEAD_DIM, HEAD_DIM)
        second = pl.multiple_of(g * 2 * HEAD_DIM + HEAD_DIM, HEAD_DIM)
        ref[:, pl.ds(first, HEAD_DIM)] = value[:ROWS].astype(ref.dtype)
        ref[:, pl.ds(second, HEAD_DIM)] = value[ROWS:].astype(ref.dtype)

    def probs_of(m, g):
        columns = pl.ds(pl.multiple_of(g * HEAD_DIM, HEAD_DIM), HEAD_DIM)
        keys = span[0, m, :, columns]
        values = span[1, m, :, columns]
        queries = pair_of(q_ref, (m,), g)
        scores = last_last(keys, queries) * score_scale + bias[m]
        weights = jnp.exp(scores - jnp.max(scores, axis=0, keepdims=True))
        probs = weights * (1.0 / jnp.sum(weights, axis=0, keepdims=True))
        return keys, values, queries, probs

    def backward(g, carry):
        keys, values, queries, probs = probs_of(1, g)
        columns = pl.ds(pl.multiple_of(g * HEAD_DIM, HEAD_DIM), HEAD_DIM)
        grads = pair_of(do_ref, (), g)
        rounded = probs.astype(jnp.bfloat16)
        grad_probs = last_last(values, grads)
        delta = jnp.sum(probs * grad_probs, axis=0, keepdims=True)
        grad_scores = (probs * score_scale * (grad_probs - delta)).astype(jnp.bfloat16)
        store_pair(dq, g, first_first(grad_scores, keys))
        for kv, terms in enumerate(
            (
                jnp.dot(grad_scores, queries, preferred_element_type=jnp.float32),
                jnp.dot(rounded, grads, preferred_element_type=jnp.float32),
            )
        ):
            far[kv, :, columns] = terms[0:ROWS].astype(jnp.bfloat16)
            near[kv, :, columns] = terms[ROWS:WINDOW].astype(jnp.bfloat16)
            own[kv, :, columns] = terms[WINDOW:]
        return carry

    def forward(g, carry):
        _, values, _, probs = probs_of(0, g)
        store_pair(att, g, first_first(probs.astype(jnp.bfloat16), values))
        return carry

    q_wide = q_ref.shape[-1] // 2
    half_heads = kv_heads // 2

    def q_half(ref, h):
        return ref.at[:, pl.ds(h * q_wide, q_wide)]

    def send_near(h):
        for kv in range(2):
            t = h * 2 + kv
            copy(
                terms_at(near, t, all_rows),
                terms_at(mate_near, t, all_rows),
                f_send.at[t],
                f_recv.at[t],
                mate,
            ).start()

    def send_queries(h):
        @pl.when(turns)
        def _():
            copy(
                q_half(dq, h),
                turned.at[h],
                s_send.at[2 + h],
                t_recv.at[h],
                (me, sec + RUN - 1),
            ).start()

        @pl.when(jnp.logical_not(turns))
        def _():
            copy(
                q_half(dq, h), q_half(dq_out, h), s_send.at[2 + h], s_recv.at[2 + h], before
            ).start()

    def turn(h):
        @pl.when(corner)
        def _():
            arrived(turned.at[h], t_recv.at[h])
            copy(
                turned.at[h],
                q_half(dq_out, h),
                t_send.at[h],
                s_recv.at[2 + h],
                (me, sec - RUN),
            ).start()

    def send_attended(h):
        copy(q_half(att, h), q_half(att_out, h), s_send.at[h], s_recv.at[h], after).start()

    back_crossing = (y == 0) & has_prev

    def send_far(t):
        h, kv = TERMS[t]
        arrived(terms_at(mate_near, t, all_rows), f_recv.at[t])

        @pl.when(core == 1)
        def _():
            lanes = slice(h * wide, (h + 1) * wide)
            far[kv, :, lanes] = (
                far[kv, :, lanes].astype(jnp.float32)
                + mate_near[kv, :, lanes].astype(jnp.float32)
            ).astype(jnp.bfloat16)

        @pl.when(y > 0)
        def _():
            copy(
                terms_at(far, t, all_rows),
                terms_at(got, t, all_rows),
                g_send.at[t],
                g_recv.at[t],
                at(top, y - 1),
            ).start()

        @pl.when(back_crossing)
        def _():
            for q in range(1, COLUMNS):
                copy(
                    terms_at(far, t, piece(q)),
                    back_a.at[t],
                    ba_send.at[t, q],
                    ba_recv.at[t],
                    at(top, q),
                ).start()
            copy(
                terms_at(far, t, piece(0)),
                back_b.at[t],
                bb_send.at[t],
                bb_recv.at[t],
                at(top - 1, 0),
            ).start()

    def relay_back_b(t):
        @pl.when((y > 0) & has_prev)
        def _():
            arrived(back_a.at[t], ba_recv.at[t])

            @pl.when(y == last)
            def _():
                copy(
                    back_a.at[t],
                    terms_at(got, t, piece(last)),
                    bb_send.at[t],
                    bb_recv.at[t],
                    at(top - 1, y),
                ).start()

            @pl.when(y < last)
            def _():
                copy(
                    back_a.at[t], back_b.at[t], bb_send.at[t], bb_recv.at[t], at(top - 1, y)
                ).start()

    def relay_back_c(t):
        @pl.when((y < last) & has_next)
        def _():
            arrived(back_b.at[t], bb_recv.at[t])
            for q in range(last):

                @pl.when(y == q)
                def _():
                    copy(
                        back_b.at[t],
                        terms_at(got, t, piece(q)),
                        bc_send.at[t],
                        bc_recv.at[t, q],
                        at(top, last),
                    ).start()

    outs = (dk_out, dv_out)

    def finish_near(t):
        @pl.when(y < last)
        def _():
            arrived(terms_at(got, t, all_rows), g_recv.at[t])
            finish(t)

    def finish_across(t):
        @pl.when(y == last)
        def _():
            @pl.when(has_next)
            def _():
                arrived(terms_at(got, t, piece(last)), bb_recv.at[t])
                for q in range(last):
                    arrived(terms_at(got, t, piece(q)), bc_recv.at[t, q])

            finish(t)

    def finish(t):
        h, kv = TERMS[t]
        lanes = slice(h * wide, (h + 1) * wide)
        total = own[kv, :, lanes] + got[kv, :, lanes].astype(jnp.float32)

        @pl.when(core == 0)
        def _():
            final[kv, :, lanes] = (total + mate_near[kv, :, lanes].astype(jnp.float32)).astype(
                jnp.bfloat16
            )

        @pl.when(core == 1)
        def _():
            final[kv, :, lanes] = total.astype(jnp.bfloat16)

        copy(
            terms_at(final, t, all_rows),
            outs[kv].at[:, half(h)],
            s_send.at[4 + t],
            s_recv.at[4 + t],
            before,
        ).start()

    for c in range(8):
        relay_b(c)
    for c in (0, 1):
        relay_c(c)
    for c in (0, 1):
        pass_on(c)
    for c in (0, 1):
        span_ready(c)
    lax.fori_loop(0, half_heads, backward, 0)
    send_near(0)
    send_queries(0)
    for c in (2, 3):
        relay_c(c)
    for c in (2, 3):
        pass_on(c)
    for t in (0, 1):
        send_far(t)
    for c in (2, 3):
        span_ready(c)
    lax.fori_loop(half_heads, kv_heads, backward, 0)
    send_near(1)
    send_queries(1)
    for t in (0, 1):
        relay_back_b(t)
    for t in (2, 3):
        send_far(t)
    for c in (4, 5):
        relay_c(c)
    for t in (2, 3):
        relay_back_b(t)
    for c in (6, 7):
        relay_c(c)
    turn(0)
    for c in (4, 5):
        pass_on(c)
    for c in (4, 5):
        span_ready(c)
    lax.fori_loop(0, half_heads, forward, 0)
    send_attended(0)
    for t in (0, 1):
        finish_near(t)
    for t in (0, 1):
        relay_back_c(t)
    for c in (6, 7):
        pass_on(c)
    for c in (6, 7):
        span_ready(c)
    lax.fori_loop(half_heads, kv_heads, forward, 0)
    send_attended(1)
    for t in (2, 3):
        finish_near(t)
    turn(1)
    for t in (2, 3):
        relay_back_c(t)
    for t in range(4):
        finish_across(t)

    for c in range(len(CHUNKS)):

        @pl.when(crossing)
        def _():
            for q in range(last):
                sent(source(c, piece(q)), a_send.at[c, q])

        @pl.when(has_next)
        def _():
            sent(rel_a.at[c], b_send.at[c])

        @pl.when(y < last)
        def _():
            sent(source(c, all_rows), r_send.at[c])

        @pl.when((y > 0) & has_prev)
        def _():
            sent(rel_b.at[c], c_send.at[c])

        @pl.when((core == 0) | (me >= 2))
        def _():
            sent(source(c, all_rows), e_send.at[c])

    for t in range(len(TERMS)):
        sent(terms_at(near, t, all_rows), f_send.at[t])

        @pl.when(y > 0)
        def _():
            sent(terms_at(far, t, all_rows), g_send.at[t])

        @pl.when(back_crossing)
        def _():
            for q in range(1, COLUMNS):
                sent(terms_at(far, t, piece(q)), ba_send.at[t, q])

        @pl.when(has_prev)
        def _():
            sent(back_a.at[t], bb_send.at[t])

        @pl.when((y < last) & has_next)
        def _():
            sent(back_b.at[t], bc_send.at[t])

    @pl.when(corner)
    def _():
        for h in range(2):
            sent(turned.at[h], t_send.at[h])

    moved = [(q_half(att, h), q_half(att_out, h)) for h in range(2)]
    moved += [(q_half(dq, h), q_half(dq_out, h)) for h in range(2)]
    moved += [(terms_at(final, t, all_rows), outs[t % 2].at[:, half(t // 2)]) for t in range(4)]
    for i, (src, dst) in enumerate(moved):
        sent(src, s_send.at[i])
        arrived(dst, s_recv.at[i])


def shards(tops, sections, queries, keys, values, out_grad, segments):
    q_width = queries.shape[-1]
    k_width = keys.shape[-1]
    kv_heads = k_width // HEAD_DIM
    half, full = jnp.bfloat16, jnp.float32
    vmem = pl.BlockSpec(memory_space=pltpu.VMEM)
    hbm = pl.BlockSpec(memory_space=pl.ANY)
    dma = pltpu.SemaphoreType.DMA
    results = pl.pallas_call(
        functools.partial(kernel, tops, sections, kv_heads),
        out_shape=[
            pltpu.VMEM((ROWS, q_width), half),
            pltpu.VMEM((ROWS, q_width), half),
            pltpu.VMEM((ROWS, k_width), half),
            pltpu.VMEM((ROWS, k_width), half),
        ],
        in_specs=[vmem, hbm, hbm, vmem, vmem],
        out_specs=[hbm] * 4,
        scratch_shapes=[
            pltpu.VMEM((2, 2, WINDOW + ROWS, k_width), half),
            pltpu.VMEM((2, WINDOW + ROWS, 2 * ROWS), full),
            pltpu.VMEM((ROWS, q_width), half),
            pltpu.VMEM((ROWS, q_width), half),
            pltpu.VMEM((2, ROWS, k_width), half),
            pltpu.VMEM((2, ROWS, k_width), half),
            pltpu.VMEM((2, ROWS, k_width), full),
            pltpu.VMEM((2, ROWS, k_width), half),
            pltpu.VMEM((2, ROWS, k_width), half),
            pltpu.VMEM((2, ROWS, k_width), half),
            pltpu.VMEM((8, PIECE, k_width // 2), half),
            pltpu.VMEM((8, PIECE, k_width // 2), half),
            pltpu.VMEM((4, PIECE, k_width // 2), half),
            pltpu.VMEM((4, PIECE, k_width // 2), half),
            dma((4,)),
            dma((8,)),
            dma((8,)),
            dma((8, COLUMNS)),
            dma((8,)),
            dma((8,)),
            dma((8,)),
            dma((8,)),
            dma((8, COLUMNS)),
            dma((8,)),
            dma((8,)),
            dma((4,)),
            dma((4,)),
            dma((4,)),
            dma((4,)),
            dma((4, COLUMNS)),
            dma((4,)),
            dma((4,)),
            dma((4,)),
            dma((4,)),
            dma((4, COLUMNS)),
            dma((8,)),
            dma((8,)),
            pltpu.VMEM((2, ROWS, q_width // 2), half),
            dma((2,)),
            dma((2,)),
        ],
        compiler_params=pltpu.CompilerParams(collective_id=0, has_side_effects=True),
    )(queries[0], keys[0], values[0], out_grad[0], segments)
    return tuple(result[None] for result in results)


def solution(mesh):
    tops = mesh.shape["seq"] // (2 * COLUMNS)
    sections = mesh.shape["section"]
    return jax.shard_map(
        functools.partial(shards, tops, sections),
        mesh=mesh,
        in_specs=(
            P("section", None, "seq", None),
            P("section", None, "seq", None),
            P("section", None, "seq", None),
            P("section", "seq", None),
            P(),
        ),
        out_specs=(
            P("section", "seq", None),
            P("section", "seq", None),
            P("section", "seq", None),
            P("section", "seq", None),
        ),
        check_vma=False,
    )
```

```python
import functools

import jax
import jax.numpy as jnp
from jax import lax
from jax.experimental import pallas as pl
from jax.experimental.pallas import tpu as pltpu
from jax.sharding import PartitionSpec as P

HEAD_DIM = 128
WINDOW = 256
ROWS = 128
COLUMNS = 4
RUN = 4
PIECE = ROWS // COLUMNS
MESH = pl.DeviceIdType.MESH

score_scale = 168.0 ** (-0.5)
masked_score = -1e30

CHUNKS = tuple((m, h, kv) for m in (1, 0) for h in range(2) for kv in range(2))
TERMS = tuple((h, kv) for h in range(2) for kv in range(2))


def last_last(a, b):
    return lax.dot_general(a, b, (((1,), (1,)), ((), ())), preferred_element_type=jnp.float32)


def first_first(a, b):
    return lax.dot_general(a, b, (((0,), (0,)), ((), ())), preferred_element_type=jnp.float32)


def kernel(
    tops,
    sections,
    kv_heads,
    q_ref,
    k_ref,
    v_ref,
    do_ref,
    seg_ref,
    att_out,
    dq_out,
    dk_out,
    dv_out,
    span,
    bias,
    att,
    dq,
    near,
    far,
    own,
    mate_near,
    got,
    final,
    rel_a,
    rel_b,
    back_a,
    back_b,
    loc_sem,
    r_send,
    r_recv,
    a_send,
    a_recv,
    b_send,
    b_recv,
    c_send,
    c_recv,
    e_send,
    e_recv,
    f_send,
    f_recv,
    g_send,
    g_recv,
    ba_send,
    ba_recv,
    bb_send,
    bb_recv,
    bc_send,
    bc_recv,
    s_send,
    s_recv,
    turned,
    t_send,
    t_recv,
):
    me = lax.axis_index("seq")
    sec = lax.axis_index("section")
    core = lax.rem(me, 2)
    y = lax.rem(lax.div(me, 2), COLUMNS)
    top = lax.div(me, 2 * COLUMNS)
    last = COLUMNS - 1

    def at(top_of, y_of):
        return ((top_of * COLUMNS + y_of) * 2 + core, sec)

    mate = (me + 1 - 2 * core, sec)
    after = (me, lax.rem(sec + 1, sections))
    before = (me, lax.rem(sec + sections - 1, sections))
    x = lax.rem(sec, RUN)
    low = lax.div(sec, RUN)
    lows = sections // RUN
    turns = (x == 0) & (low > 0)
    corner = (x == RUN - 1) & (low > 0)
    corner_after = (x == RUN - 1) & (low < lows - 1)
    has_next = top < tops - 1
    has_prev = top > 0

    def copy(src, dst, send, recv, device):
        return pltpu.make_async_remote_copy(
            src_ref=src,
            dst_ref=dst,
            send_sem=send,
            recv_sem=recv,
            device_id=device,
            device_id_type=MESH,
        )

    def arrived(dst, recv):
        copy(dst, dst, e_send.at[0], recv, mate).wait_recv()

    def sent(src, send):
        copy(src, src, send, e_recv.at[0], mate).wait_send()

    sources = (k_ref, v_ref)
    wide = k_ref.shape[-1] // 2
    all_rows = pl.ds(0, ROWS)
    near_rows = pl.ds(ROWS, ROWS)

    def piece(q):
        return pl.ds(q * PIECE, PIECE)

    def half(h):
        return pl.ds(h * wide, wide)

    def source(c, rows):
        m, h, kv = CHUNKS[c]
        return sources[kv].at[m, rows, half(h)]

    def spot(c, rows):
        m, h, kv = CHUNKS[c]
        return span.at[kv, m, rows, half(h)]

    def terms_at(ref, t, rows):
        h, kv = TERMS[t]
        return ref.at[kv, rows, half(h)]

    def loads(m, kv):
        return pltpu.make_async_copy(
            sources[kv].at[m], span.at[kv, m, pl.ds(WINDOW, ROWS)], loc_sem.at[m * 2 + kv]
        )

    @pl.when(me == 0)
    def _():
        span[:, :, 0:WINDOW, :] = jnp.zeros((2, 2, WINDOW, span.shape[3]), span.dtype)

    @pl.when(me == 1)
    def _():
        span[:, :, 0:ROWS, :] = jnp.zeros((2, 2, ROWS, span.shape[3]), span.dtype)

    @pl.when(me >= tops * 2 * COLUMNS - 2)
    def _():
        got[...] = jnp.zeros_like(got)

    for m in (1, 0):
        for kv in range(2):
            loads(m, kv).start()

    barrier = pltpu.get_barrier_semaphore()
    pl.semaphore_signal(barrier, inc=1, device_id=mate, device_id_type=MESH)
    pl.semaphore_signal(barrier, inc=1, device_id=after, device_id_type=MESH)
    pl.semaphore_signal(barrier, inc=1, device_id=before, device_id_type=MESH)
    for step in range(1, COLUMNS):
        pl.semaphore_signal(
            barrier,
            inc=1,
            device_id=at(top, lax.rem(y + step, COLUMNS)),
            device_id_type=MESH,
        )


    @pl.when(has_next)
    def _():
        pl.semaphore_signal(barrier, inc=1, device_id=at(top + 1, y), device_id_type=MESH)

    @pl.when(has_prev)
    def _():
        pl.semaphore_signal(barrier, inc=1, device_id=at(top - 1, y), device_id_type=MESH)

    def greet(condition, section):
        @pl.when(condition)
        def _():
            pl.semaphore_signal(barrier, inc=1, device_id=(me, section), device_id_type=MESH)

    greet(turns, sec + RUN - 1)
    greet(corner, sec - RUN + 1)
    greet(corner, sec - RUN)
    greet(corner_after, sec + RUN)

    column_of = lax.broadcasted_iota(jnp.int32, (ROWS, ROWS), 1)
    row_of = lax.broadcasted_iota(jnp.int32, (ROWS, ROWS), 0)
    for m in range(2):
        here = pl.ds(pl.multiple_of(me * ROWS, ROWS), ROWS)
        seg_query = jnp.broadcast_to(seg_ref[m : m + 1, here].astype(jnp.float32), (ROWS, ROWS))
        for part in range(3):
            block = jnp.maximum(me - 2 + part, 0)
            there = pl.ds(pl.multiple_of(block * ROWS, ROWS), ROWS)
            seg_key = jnp.broadcast_to(seg_ref[m : m + 1, there].astype(jnp.float32), (ROWS, ROWS)).T
            offset = column_of + WINDOW - part * ROWS - row_of
            allowed = (seg_query == seg_key) & (offset >= 0) & (offset < WINDOW)
            allowed = allowed & (row_of + (part - 2 + me) * ROWS >= 0)
            value = jnp.where(allowed, 0.0, masked_score)
            bias[m, part * ROWS : (part + 1) * ROWS, 0:ROWS] = value
            bias[m, part * ROWS : (part + 1) * ROWS, ROWS : 2 * ROWS] = value

    across = jnp.minimum(top, 1) + jnp.minimum(tops - 1 - top, 1)
    first, final_x = 1 - jnp.minimum(x, 1), jnp.maximum(x - (RUN - 2), 0)
    behind, ahead = jnp.minimum(low, 1), jnp.minimum(lows - 1 - low, 1)
    turning = first * behind + final_x * (2 * behind + ahead)
    pl.semaphore_wait(barrier, 3 + COLUMNS - 1 + across + turning)

    def halo_b(c, src):
        @pl.when(y == 0)
        def _():
            copy(src, spot(c, piece(0)), b_send.at[c], b_recv.at[c], at(top + 1, y)).start()

        @pl.when(y > 0)
        def _():
            copy(src, rel_b.at[c], b_send.at[c], b_recv.at[c], at(top + 1, y)).start()

    crossing = (y == last) & has_next
    for c in range(len(CHUNKS)):

        @pl.when(crossing)
        def _():
            for q in range(last):
                copy(
                    source(c, piece(q)), rel_a.at[c], a_send.at[c, q], a_recv.at[c], at(top, q)
                ).start()
            copy(
                source(c, piece(last)), rel_b.at[c], b_send.at[c], b_recv.at[c], at(top + 1, last)
            ).start()

        @pl.when(y < last)
        def _():
            copy(
                source(c, all_rows), spot(c, all_rows), r_send.at[c], r_recv.at[c], at(top, y + 1)
            ).start()

        @pl.when(core == 0)
        def _():
            copy(
                source(c, all_rows), spot(c, near_rows), e_send.at[c], e_recv.at[c], mate
            ).start()

    def relay_b(c):
        @pl.when((y < last) & has_next)
        def _():
            arrived(rel_a.at[c], a_recv.at[c])
            halo_b(c, rel_a.at[c])

    def relay_c(c):
        @pl.when((y > 0) & has_prev)
        def _():
            arrived(rel_b.at[c], b_recv.at[c])
            for q in range(1, COLUMNS):

                @pl.when(y == q)
                def _():
                    copy(
                        rel_b.at[c], spot(c, piece(q)), c_send.at[c], c_recv.at[c, q], at(top, 0)
                    ).start()

    def pass_on(c):
        @pl.when((y == 0) & has_prev)
        def _():
            arrived(spot(c, piece(0)), b_recv.at[c])
            for q in range(1, COLUMNS):
                arrived(spot(c, piece(q)), c_recv.at[c, q])

        @pl.when(y > 0)
        def _():
            arrived(spot(c, all_rows), r_recv.at[c])

        @pl.when((core == 1) & (me >= 2))
        def _():
            copy(
                spot(c, all_rows), spot(c, near_rows), e_send.at[c], e_recv.at[c], mate
            ).start()

    def span_ready(c):
        m, h, kv = CHUNKS[c]

        @pl.when(me > 0)
        def _():
            arrived(spot(c, near_rows), e_recv.at[c])

        if h == 0:
            loads(m, kv).wait()

    def pair_of(ref, index, g):
        first = pl.multiple_of(g * 2 * HEAD_DIM, HEAD_DIM)
        second = pl.multiple_of(g * 2 * HEAD_DIM + HEAD_DIM, HEAD_DIM)
        return jnp.concatenate(
            [
                ref[index + (slice(None), pl.ds(first, HEAD_DIM))],
                ref[index + (slice(None), pl.ds(second, HEAD_DIM))],
            ],
            axis=0,
        )

    def store_pair(ref, g, value):
        first = pl.multiple_of(g * 2 * HEAD_DIM, HEAD_DIM)
        second = pl.multiple_of(g * 2 * HEAD_DIM + HEAD_DIM, HEAD_DIM)
        ref[:, pl.ds(first, HEAD_DIM)] = value[:ROWS].astype(ref.dtype)
        ref[:, pl.ds(second, HEAD_DIM)] = value[ROWS:].astype(ref.dtype)

    def probs_of(m, g):
        columns = pl.ds(pl.multiple_of(g * HEAD_DIM, HEAD_DIM), HEAD_DIM)
        keys = span[0, m, :, columns]
        values = span[1, m, :, columns]
        queries = pair_of(q_ref, (m,), g)
        scores = last_last(keys, queries) * score_scale + bias[m]
        weights = jnp.exp(scores - jnp.max(scores, axis=0, keepdims=True))
        probs = weights * (1.0 / jnp.sum(weights, axis=0, keepdims=True))
        return keys, values, queries, probs

    def backward(g, carry):
        keys, values, queries, probs = probs_of(1, g)
        columns = pl.ds(pl.multiple_of(g * HEAD_DIM, HEAD_DIM), HEAD_DIM)
        grads = pair_of(do_ref, (), g)
        rounded = probs.astype(jnp.bfloat16)
        grad_probs = last_last(values, grads)
        delta = jnp.sum(probs * grad_probs, axis=0, keepdims=True)
        grad_scores = (probs * score_scale * (grad_probs - delta)).astype(jnp.bfloat16)
        store_pair(dq, g, first_first(grad_scores, keys))
        for kv, terms in enumerate(
            (
                jnp.dot(grad_scores, queries, preferred_element_type=jnp.float32),
                jnp.dot(rounded, grads, preferred_element_type=jnp.float32),
            )
        ):
            far[kv, :, columns] = terms[0:ROWS].astype(jnp.bfloat16)
            near[kv, :, columns] = terms[ROWS:WINDOW].astype(jnp.bfloat16)
            own[kv, :, columns] = terms[WINDOW:]
        return carry

    def forward(g, carry):
        _, values, _, probs = probs_of(0, g)
        store_pair(att, g, first_first(probs.astype(jnp.bfloat16), values))
        return carry

    q_wide = q_ref.shape[-1] // 2
    half_heads = kv_heads // 2

    def q_half(ref, h):
        return ref.at[:, pl.ds(h * q_wide, q_wide)]

    def send_near(h):
        for kv in range(2):
            t = h * 2 + kv
            copy(
                terms_at(near, t, all_rows),
                terms_at(mate_near, t, all_rows),
                f_send.at[t],
                f_recv.at[t],
                mate,
            ).start()

    def send_queries(h):
        @pl.when(turns)
        def _():
            copy(
                q_half(dq, h),
                turned.at[h],
                s_send.at[2 + h],
                t_recv.at[h],
                (me, sec + RUN - 1),
            ).start()

        @pl.when(jnp.logical_not(turns))
        def _():
            copy(
                q_half(dq, h), q_half(dq_out, h), s_send.at[2 + h], s_recv.at[2 + h], before
            ).start()

    def turn(h):
        @pl.when(corner)
        def _():
            arrived(turned.at[h], t_recv.at[h])
            copy(
                turned.at[h],
                q_half(dq_out, h),
                t_send.at[h],
                s_recv.at[2 + h],
                (me, sec - RUN),
            ).start()

    def send_attended(h):
        copy(q_half(att, h), q_half(att_out, h), s_send.at[h], s_recv.at[h], after).start()

    back_crossing = (y == 0) & has_prev

    def send_far(t):
        h, kv = TERMS[t]
        arrived(terms_at(mate_near, t, all_rows), f_recv.at[t])

        @pl.when(core == 1)
        def _():
            lanes = slice(h * wide, (h + 1) * wide)
            far[kv, :, lanes] = (
                far[kv, :, lanes].astype(jnp.float32)
                + mate_near[kv, :, lanes].astype(jnp.float32)
            ).astype(jnp.bfloat16)

        @pl.when(y > 0)
        def _():
            copy(
                terms_at(far, t, all_rows),
                terms_at(got, t, all_rows),
                g_send.at[t],
                g_recv.at[t],
                at(top, y - 1),
            ).start()

        @pl.when(back_crossing)
        def _():
            for q in range(1, COLUMNS):
                copy(
                    terms_at(far, t, piece(q)),
                    back_a.at[t],
                    ba_send.at[t, q],
                    ba_recv.at[t],
                    at(top, q),
                ).start()
            copy(
                terms_at(far, t, piece(0)),
                back_b.at[t],
                bb_send.at[t],
                bb_recv.at[t],
                at(top - 1, 0),
            ).start()

    def relay_back_b(t):
        @pl.when((y > 0) & has_prev)
        def _():
            arrived(back_a.at[t], ba_recv.at[t])

            @pl.when(y == last)
            def _():
                copy(
                    back_a.at[t],
                    terms_at(got, t, piece(last)),
                    bb_send.at[t],
                    bb_recv.at[t],
                    at(top - 1, y),
                ).start()

            @pl.when(y < last)
            def _():
                copy(
                    back_a.at[t], back_b.at[t], bb_send.at[t], bb_recv.at[t], at(top - 1, y)
                ).start()

    def relay_back_c(t):
        @pl.when((y < last) & has_next)
        def _():
            arrived(back_b.at[t], bb_recv.at[t])
            for q in range(last):

                @pl.when(y == q)
                def _():
                    copy(
                        back_b.at[t],
                        terms_at(got, t, piece(q)),
                        bc_send.at[t],
                        bc_recv.at[t, q],
                        at(top, last),
                    ).start()

    outs = (dk_out, dv_out)

    def finish_near(t):
        @pl.when(y < last)
        def _():
            arrived(terms_at(got, t, all_rows), g_recv.at[t])
            finish(t)

    def finish_across(t):
        @pl.when(y == last)
        def _():
            @pl.when(has_next)
            def _():
                arrived(terms_at(got, t, piece(last)), bb_recv.at[t])
                for q in range(last):
                    arrived(terms_at(got, t, piece(q)), bc_recv.at[t, q])

            finish(t)

    def finish(t):
        h, kv = TERMS[t]
        lanes = slice(h * wide, (h + 1) * wide)
        total = own[kv, :, lanes] + got[kv, :, lanes].astype(jnp.float32)

        @pl.when(core == 0)
        def _():
            final[kv, :, lanes] = (total + mate_near[kv, :, lanes].astype(jnp.float32)).astype(
                jnp.bfloat16
            )

        @pl.when(core == 1)
        def _():
            final[kv, :, lanes] = total.astype(jnp.bfloat16)

        copy(
            terms_at(final, t, all_rows),
            outs[kv].at[:, half(h)],
            s_send.at[4 + t],
            s_recv.at[4 + t],
            before,
        ).start()

    for c in range(8):
        relay_b(c)
    for c in (0, 1):
        relay_c(c)
    for c in (0, 1):
        pass_on(c)
    for c in (0, 1):
        span_ready(c)
    lax.fori_loop(0, half_heads, backward, 0)
    send_near(0)
    send_queries(0)
    for c in (2, 3):
        relay_c(c)
    for c in (2, 3):
        pass_on(c)
    for t in (0, 1):
        send_far(t)
    for c in (2, 3):
        span_ready(c)
    lax.fori_loop(half_heads, kv_heads, backward, 0)
    send_near(1)
    send_queries(1)
    for t in (0, 1):
        relay_back_b(t)
    for t in (2, 3):
        send_far(t)
    for t in (2, 3):
        relay_back_b(t)
    for c in (4, 5):
        relay_c(c)
    for c in (6, 7):
        relay_c(c)
    turn(0)
    for c in (4, 5):
        pass_on(c)
    for c in (4, 5):
        span_ready(c)
    lax.fori_loop(0, half_heads, forward, 0)
    send_attended(0)
    for t in (0, 1):
        finish_near(t)
    for t in (0, 1):
        relay_back_c(t)
    for c in (6, 7):
        pass_on(c)
    for c in (6, 7):
        span_ready(c)
    lax.fori_loop(half_heads, kv_heads, forward, 0)
    send_attended(1)
    for t in (2, 3):
        finish_near(t)
    turn(1)
    for t in (2, 3):
        relay_back_c(t)
    for t in range(4):
        finish_across(t)

    for c in range(len(CHUNKS)):

        @pl.when(crossing)
        def _():
            for q in range(last):
                sent(source(c, piece(q)), a_send.at[c, q])

        @pl.when(has_next)
        def _():
            sent(rel_a.at[c], b_send.at[c])

        @pl.when(y < last)
        def _():
            sent(source(c, all_rows), r_send.at[c])

        @pl.when((y > 0) & has_prev)
        def _():
            sent(rel_b.at[c], c_send.at[c])

        @pl.when((core == 0) | (me >= 2))
        def _():
            sent(source(c, all_rows), e_send.at[c])

    for t in range(len(TERMS)):
        sent(terms_at(near, t, all_rows), f_send.at[t])

        @pl.when(y > 0)
        def _():
            sent(terms_at(far, t, all_rows), g_send.at[t])

        @pl.when(back_crossing)
        def _():
            for q in range(1, COLUMNS):
                sent(terms_at(far, t, piece(q)), ba_send.at[t, q])

        @pl.when(has_prev)
        def _():
            sent(back_a.at[t], bb_send.at[t])

        @pl.when((y < last) & has_next)
        def _():
            sent(back_b.at[t], bc_send.at[t])

    @pl.when(corner)
    def _():
        for h in range(2):
            sent(turned.at[h], t_send.at[h])

    moved = [(q_half(att, h), q_half(att_out, h)) for h in range(2)]
    moved += [(q_half(dq, h), q_half(dq_out, h)) for h in range(2)]
    moved += [(terms_at(final, t, all_rows), outs[t % 2].at[:, half(t // 2)]) for t in range(4)]
    for i, (src, dst) in enumerate(moved):
        sent(src, s_send.at[i])
        arrived(dst, s_recv.at[i])


def shards(tops, sections, queries, keys, values, out_grad, segments):
    q_width = queries.shape[-1]
    k_width = keys.shape[-1]
    kv_heads = k_width // HEAD_DIM
    half, full = jnp.bfloat16, jnp.float32
    vmem = pl.BlockSpec(memory_space=pltpu.VMEM)
    hbm = pl.BlockSpec(memory_space=pl.ANY)
    dma = pltpu.SemaphoreType.DMA
    results = pl.pallas_call(
        functools.partial(kernel, tops, sections, kv_heads),
        out_shape=[
            pltpu.VMEM((ROWS, q_width), half),
            pltpu.VMEM((ROWS, q_width), half),
            pltpu.VMEM((ROWS, k_width), half),
            pltpu.VMEM((ROWS, k_width), half),
        ],
        in_specs=[vmem, hbm, hbm, vmem, vmem],
        out_specs=[hbm] * 4,
        scratch_shapes=[
            pltpu.VMEM((2, 2, WINDOW + ROWS, k_width), half),
            pltpu.VMEM((2, WINDOW + ROWS, 2 * ROWS), full),
            pltpu.VMEM((ROWS, q_width), half),
            pltpu.VMEM((ROWS, q_width), half),
            pltpu.VMEM((2, ROWS, k_width), half),
            pltpu.VMEM((2, ROWS, k_width), half),
            pltpu.VMEM((2, ROWS, k_width), full),
            pltpu.VMEM((2, ROWS, k_width), half),
            pltpu.VMEM((2, ROWS, k_width), half),
            pltpu.VMEM((2, ROWS, k_width), half),
            pltpu.VMEM((8, PIECE, k_width // 2), half),
            pltpu.VMEM((8, PIECE, k_width // 2), half),
            pltpu.VMEM((4, PIECE, k_width // 2), half),
            pltpu.VMEM((4, PIECE, k_width // 2), half),
            dma((4,)),
            dma((8,)),
            dma((8,)),
            dma((8, COLUMNS)),
            dma((8,)),
            dma((8,)),
            dma((8,)),
            dma((8,)),
            dma((8, COLUMNS)),
            dma((8,)),
            dma((8,)),
            dma((4,)),
            dma((4,)),
            dma((4,)),
            dma((4,)),
            dma((4, COLUMNS)),
            dma((4,)),
            dma((4,)),
            dma((4,)),
            dma((4,)),
            dma((4, COLUMNS)),
            dma((8,)),
            dma((8,)),
            pltpu.VMEM((2, ROWS, q_width // 2), half),
            dma((2,)),
            dma((2,)),
        ],
        compiler_params=pltpu.CompilerParams(collective_id=0, has_side_effects=True),
    )(queries[0], keys[0], values[0], out_grad[0], segments)
    return tuple(result[None] for result in results)


def solution(mesh):
    tops = mesh.shape["seq"] // (2 * COLUMNS)
    sections = mesh.shape["section"]
    return jax.shard_map(
        functools.partial(shards, tops, sections),
        mesh=mesh,
        in_specs=(
            P("section", None, "seq", None),
            P("section", None, "seq", None),
            P("section", None, "seq", None),
            P("section", "seq", None),
            P(),
        ),
        out_specs=(
            P("section", "seq", None),
            P("section", "seq", None),
            P("section", "seq", None),
            P("section", "seq", None),
        ),
        check_vma=False,
    )
```

```python
import functools

import jax
import jax.numpy as jnp
from jax import lax
from jax.experimental import pallas as pl
from jax.experimental.pallas import tpu as pltpu
from jax.sharding import PartitionSpec as P

HEAD_DIM = 128
WINDOW = 256
ROWS = 128
COLUMNS = 4
RUN = 4
PIECE = ROWS // COLUMNS
MESH = pl.DeviceIdType.MESH

score_scale = 168.0 ** (-0.5)
masked_score = -1e30

CHUNKS = tuple((m, h, kv) for m in (1, 0) for h in range(2) for kv in range(2))
TERMS = tuple((h, kv) for h in range(2) for kv in range(2))


def last_last(a, b):
    return lax.dot_general(a, b, (((1,), (1,)), ((), ())), preferred_element_type=jnp.float32)


def first_first(a, b):
    return lax.dot_general(a, b, (((0,), (0,)), ((), ())), preferred_element_type=jnp.float32)


def kernel(
    tops,
    sections,
    kv_heads,
    q_ref,
    k_ref,
    v_ref,
    do_ref,
    seg_ref,
    att_out,
    dq_out,
    dk_out,
    dv_out,
    span,
    bias,
    att,
    dq,
    near,
    far,
    own,
    mate_near,
    got,
    final,
    rel_a,
    rel_b,
    back_a,
    back_b,
    loc_sem,
    r_send,
    r_recv,
    a_send,
    a_recv,
    b_send,
    b_recv,
    c_send,
    c_recv,
    e_send,
    e_recv,
    f_send,
    f_recv,
    g_send,
    g_recv,
    ba_send,
    ba_recv,
    bb_send,
    bb_recv,
    bc_send,
    bc_recv,
    s_send,
    s_recv,
    turned,
    t_send,
    t_recv,
):
    me = lax.axis_index("seq")
    sec = lax.axis_index("section")
    core = lax.rem(me, 2)
    y = lax.rem(lax.div(me, 2), COLUMNS)
    top = lax.div(me, 2 * COLUMNS)
    last = COLUMNS - 1

    def at(top_of, y_of):
        return ((top_of * COLUMNS + y_of) * 2 + core, sec)

    mate = (me + 1 - 2 * core, sec)
    after = (me, lax.rem(sec + 1, sections))
    before = (me, lax.rem(sec + sections - 1, sections))
    x = lax.rem(sec, RUN)
    low = lax.div(sec, RUN)
    lows = sections // RUN
    turns = (x == 0) & (low > 0)
    corner = (x == RUN - 1) & (low > 0)
    corner_after = (x == RUN - 1) & (low < lows - 1)
    has_next = top < tops - 1
    has_prev = top > 0

    def copy(src, dst, send, recv, device):
        return pltpu.make_async_remote_copy(
            src_ref=src,
            dst_ref=dst,
            send_sem=send,
            recv_sem=recv,
            device_id=device,
            device_id_type=MESH,
        )

    def arrived(dst, recv):
        copy(dst, dst, e_send.at[0], recv, mate).wait_recv()

    def sent(src, send):
        copy(src, src, send, e_recv.at[0], mate).wait_send()

    sources = (k_ref, v_ref)
    wide = k_ref.shape[-1] // 2
    all_rows = pl.ds(0, ROWS)
    near_rows = pl.ds(ROWS, ROWS)

    def piece(q):
        return pl.ds(q * PIECE, PIECE)

    def half(h):
        return pl.ds(h * wide, wide)

    def source(c, rows):
        m, h, kv = CHUNKS[c]
        return sources[kv].at[m, rows, half(h)]

    def spot(c, rows):
        m, h, kv = CHUNKS[c]
        return span.at[kv, m, rows, half(h)]

    def terms_at(ref, t, rows):
        h, kv = TERMS[t]
        return ref.at[kv, rows, half(h)]

    def loads(m, kv):
        return pltpu.make_async_copy(
            sources[kv].at[m], span.at[kv, m, pl.ds(WINDOW, ROWS)], loc_sem.at[m * 2 + kv]
        )

    @pl.when(me == 0)
    def _():
        span[:, :, 0:WINDOW, :] = jnp.zeros((2, 2, WINDOW, span.shape[3]), span.dtype)

    @pl.when(me == 1)
    def _():
        span[:, :, 0:ROWS, :] = jnp.zeros((2, 2, ROWS, span.shape[3]), span.dtype)

    @pl.when(me >= tops * 2 * COLUMNS - 2)
    def _():
        got[...] = jnp.zeros_like(got)

    for m in (1, 0):
        for kv in range(2):
            loads(m, kv).start()

    barrier = pltpu.get_barrier_semaphore()
    pl.semaphore_signal(barrier, inc=1, device_id=mate, device_id_type=MESH)
    pl.semaphore_signal(barrier, inc=1, device_id=after, device_id_type=MESH)
    pl.semaphore_signal(barrier, inc=1, device_id=before, device_id_type=MESH)
    for step in range(1, COLUMNS):
        pl.semaphore_signal(
            barrier,
            inc=1,
            device_id=at(top, lax.rem(y + step, COLUMNS)),
            device_id_type=MESH,
        )


    @pl.when(has_next)
    def _():
        pl.semaphore_signal(barrier, inc=1, device_id=at(top + 1, y), device_id_type=MESH)

    @pl.when(has_prev)
    def _():
        pl.semaphore_signal(barrier, inc=1, device_id=at(top - 1, y), device_id_type=MESH)

    def greet(condition, section):
        @pl.when(condition)
        def _():
            pl.semaphore_signal(barrier, inc=1, device_id=(me, section), device_id_type=MESH)

    greet(turns, sec + RUN - 1)
    greet(corner, sec - RUN + 1)
    greet(corner, sec - RUN)
    greet(corner_after, sec + RUN)

    column_of = lax.broadcasted_iota(jnp.int32, (ROWS, ROWS), 1)
    row_of = lax.broadcasted_iota(jnp.int32, (ROWS, ROWS), 0)
    for m in range(2):
        here = pl.ds(pl.multiple_of(me * ROWS, ROWS), ROWS)
        seg_query = jnp.broadcast_to(seg_ref[m : m + 1, here].astype(jnp.float32), (ROWS, ROWS))
        for part in range(3):
            block = jnp.maximum(me - 2 + part, 0)
            there = pl.ds(pl.multiple_of(block * ROWS, ROWS), ROWS)
            seg_key = jnp.broadcast_to(seg_ref[m : m + 1, there].astype(jnp.float32), (ROWS, ROWS)).T
            offset = column_of + WINDOW - part * ROWS - row_of
            allowed = (seg_query == seg_key) & (offset >= 0) & (offset < WINDOW)
            allowed = allowed & (row_of + (part - 2 + me) * ROWS >= 0)
            value = jnp.where(allowed, 0.0, masked_score)
            bias[m, part * ROWS : (part + 1) * ROWS, 0:ROWS] = value
            bias[m, part * ROWS : (part + 1) * ROWS, ROWS : 2 * ROWS] = value

    across = jnp.minimum(top, 1) + jnp.minimum(tops - 1 - top, 1)
    first, final_x = 1 - jnp.minimum(x, 1), jnp.maximum(x - (RUN - 2), 0)
    behind, ahead = jnp.minimum(low, 1), jnp.minimum(lows - 1 - low, 1)
    turning = first * behind + final_x * (2 * behind + ahead)
    pl.semaphore_wait(barrier, 3 + COLUMNS - 1 + across + turning)

    def halo_b(c, src):
        @pl.when(y == 0)
        def _():
            copy(src, spot(c, piece(0)), b_send.at[c], b_recv.at[c], at(top + 1, y)).start()

        @pl.when(y > 0)
        def _():
            copy(src, rel_b.at[c], b_send.at[c], b_recv.at[c], at(top + 1, y)).start()

    crossing = (y == last) & has_next
    for c in range(len(CHUNKS)):

        @pl.when(crossing)
        def _():
            for q in range(last):
                copy(
                    source(c, piece(q)), rel_a.at[c], a_send.at[c, q], a_recv.at[c], at(top, q)
                ).start()
            copy(
                source(c, piece(last)), rel_b.at[c], b_send.at[c], b_recv.at[c], at(top + 1, last)
            ).start()

        @pl.when(y < last)
        def _():
            copy(
                source(c, all_rows), spot(c, all_rows), r_send.at[c], r_recv.at[c], at(top, y + 1)
            ).start()

        @pl.when(core == 0)
        def _():
            copy(
                source(c, all_rows), spot(c, near_rows), e_send.at[c], e_recv.at[c], mate
            ).start()

    def relay_b(c):
        @pl.when((y < last) & has_next)
        def _():
            arrived(rel_a.at[c], a_recv.at[c])
            halo_b(c, rel_a.at[c])

    def relay_c(c):
        @pl.when((y > 0) & has_prev)
        def _():
            arrived(rel_b.at[c], b_recv.at[c])
            for q in range(1, COLUMNS):

                @pl.when(y == q)
                def _():
                    copy(
                        rel_b.at[c], spot(c, piece(q)), c_send.at[c], c_recv.at[c, q], at(top, 0)
                    ).start()

    def pass_on(c):
        @pl.when((y == 0) & has_prev)
        def _():
            arrived(spot(c, piece(0)), b_recv.at[c])
            for q in range(1, COLUMNS):
                arrived(spot(c, piece(q)), c_recv.at[c, q])

        @pl.when(y > 0)
        def _():
            arrived(spot(c, all_rows), r_recv.at[c])

        @pl.when((core == 1) & (me >= 2))
        def _():
            copy(
                spot(c, all_rows), spot(c, near_rows), e_send.at[c], e_recv.at[c], mate
            ).start()

    def span_ready(c):
        m, h, kv = CHUNKS[c]

        @pl.when(me > 0)
        def _():
            arrived(spot(c, near_rows), e_recv.at[c])

        if h == 0:
            loads(m, kv).wait()

    def pair_of(ref, index, g):
        first = pl.multiple_of(g * 2 * HEAD_DIM, HEAD_DIM)
        second = pl.multiple_of(g * 2 * HEAD_DIM + HEAD_DIM, HEAD_DIM)
        return jnp.concatenate(
            [
                ref[index + (slice(None), pl.ds(first, HEAD_DIM))],
                ref[index + (slice(None), pl.ds(second, HEAD_DIM))],
            ],
            axis=0,
        )

    def store_pair(ref, g, value):
        first = pl.multiple_of(g * 2 * HEAD_DIM, HEAD_DIM)
        second = pl.multiple_of(g * 2 * HEAD_DIM + HEAD_DIM, HEAD_DIM)
        ref[:, pl.ds(first, HEAD_DIM)] = value[:ROWS].astype(ref.dtype)
        ref[:, pl.ds(second, HEAD_DIM)] = value[ROWS:].astype(ref.dtype)

    def probs_of(m, g):
        columns = pl.ds(pl.multiple_of(g * HEAD_DIM, HEAD_DIM), HEAD_DIM)
        keys = span[0, m, :, columns]
        values = span[1, m, :, columns]
        queries = pair_of(q_ref, (m,), g)
        scores = last_last(keys, queries) * score_scale + bias[m]
        weights = jnp.exp(scores - jnp.max(scores, axis=0, keepdims=True))
        probs = weights * (1.0 / jnp.sum(weights, axis=0, keepdims=True))
        return keys, values, queries, probs

    def backward(g, carry):
        keys, values, queries, probs = probs_of(1, g)
        columns = pl.ds(pl.multiple_of(g * HEAD_DIM, HEAD_DIM), HEAD_DIM)
        grads = pair_of(do_ref, (), g)
        rounded = probs.astype(jnp.bfloat16)
        grad_probs = last_last(values, grads)
        delta = jnp.sum(probs * grad_probs, axis=0, keepdims=True)
        grad_scores = (probs * score_scale * (grad_probs - delta)).astype(jnp.bfloat16)
        store_pair(dq, g, first_first(grad_scores, keys))
        for kv, terms in enumerate(
            (
                jnp.dot(grad_scores, queries, preferred_element_type=jnp.float32),
                jnp.dot(rounded, grads, preferred_element_type=jnp.float32),
            )
        ):
            far[kv, :, columns] = terms[0:ROWS].astype(jnp.bfloat16)
            near[kv, :, columns] = terms[ROWS:WINDOW].astype(jnp.bfloat16)
            own[kv, :, columns] = terms[WINDOW:]
        return carry

    def forward(g, carry):
        _, values, _, probs = probs_of(0, g)
        store_pair(att, g, first_first(probs.astype(jnp.bfloat16), values))
        return carry

    q_wide = q_ref.shape[-1] // 2
    half_heads = kv_heads // 2

    def q_half(ref, h):
        return ref.at[:, pl.ds(h * q_wide, q_wide)]

    def send_near(h):
        for kv in range(2):
            t = h * 2 + kv
            copy(
                terms_at(near, t, all_rows),
                terms_at(mate_near, t, all_rows),
                f_send.at[t],
                f_recv.at[t],
                mate,
            ).start()

    def send_queries(h):
        @pl.when(turns)
        def _():
            copy(
                q_half(dq, h),
                turned.at[h],
                s_send.at[2 + h],
                t_recv.at[h],
                (me, sec + RUN - 1),
            ).start()

        @pl.when(jnp.logical_not(turns))
        def _():
            copy(
                q_half(dq, h), q_half(dq_out, h), s_send.at[2 + h], s_recv.at[2 + h], before
            ).start()

    def turn(h):
        @pl.when(corner)
        def _():
            arrived(turned.at[h], t_recv.at[h])
            copy(
                turned.at[h],
                q_half(dq_out, h),
                t_send.at[h],
                s_recv.at[2 + h],
                (me, sec - RUN),
            ).start()

    def send_attended(h):
        copy(q_half(att, h), q_half(att_out, h), s_send.at[h], s_recv.at[h], after).start()

    back_crossing = (y == 0) & has_prev

    def send_far(t):
        h, kv = TERMS[t]
        arrived(terms_at(mate_near, t, all_rows), f_recv.at[t])

        @pl.when(core == 1)
        def _():
            lanes = slice(h * wide, (h + 1) * wide)
            far[kv, :, lanes] = (
                far[kv, :, lanes].astype(jnp.float32)
                + mate_near[kv, :, lanes].astype(jnp.float32)
            ).astype(jnp.bfloat16)

        @pl.when(y > 0)
        def _():
            copy(
                terms_at(far, t, all_rows),
                terms_at(got, t, all_rows),
                g_send.at[t],
                g_recv.at[t],
                at(top, y - 1),
            ).start()

        @pl.when(back_crossing)
        def _():
            for q in range(1, COLUMNS):
                copy(
                    terms_at(far, t, piece(q)),
                    back_a.at[t],
                    ba_send.at[t, q],
                    ba_recv.at[t],
                    at(top, q),
                ).start()
            copy(
                terms_at(far, t, piece(0)),
                back_b.at[t],
                bb_send.at[t],
                bb_recv.at[t],
                at(top - 1, 0),
            ).start()

    def relay_back_b(t):
        @pl.when((y > 0) & has_prev)
        def _():
            arrived(back_a.at[t], ba_recv.at[t])

            @pl.when(y == last)
            def _():
                copy(
                    back_a.at[t],
                    terms_at(got, t, piece(last)),
                    bb_send.at[t],
                    bb_recv.at[t],
                    at(top - 1, y),
                ).start()

            @pl.when(y < last)
            def _():
                copy(
                    back_a.at[t], back_b.at[t], bb_send.at[t], bb_recv.at[t], at(top - 1, y)
                ).start()

    def relay_back_c(t):
        @pl.when((y < last) & has_next)
        def _():
            arrived(back_b.at[t], bb_recv.at[t])
            for q in range(last):

                @pl.when(y == q)
                def _():
                    copy(
                        back_b.at[t],
                        terms_at(got, t, piece(q)),
                        bc_send.at[t],
                        bc_recv.at[t, q],
                        at(top, last),
                    ).start()

    outs = (dk_out, dv_out)

    def finish_near(t):
        @pl.when(y < last)
        def _():
            arrived(terms_at(got, t, all_rows), g_recv.at[t])
            finish(t)

    def finish_across(t):
        @pl.when(y == last)
        def _():
            @pl.when(has_next)
            def _():
                arrived(terms_at(got, t, piece(last)), bb_recv.at[t])
                for q in range(last):
                    arrived(terms_at(got, t, piece(q)), bc_recv.at[t, q])

            finish(t)

    def finish(t):
        h, kv = TERMS[t]
        lanes = slice(h * wide, (h + 1) * wide)
        total = own[kv, :, lanes] + got[kv, :, lanes].astype(jnp.float32)

        @pl.when(core == 0)
        def _():
            final[kv, :, lanes] = (total + mate_near[kv, :, lanes].astype(jnp.float32)).astype(
                jnp.bfloat16
            )

        @pl.when(core == 1)
        def _():
            final[kv, :, lanes] = total.astype(jnp.bfloat16)

        copy(
            terms_at(final, t, all_rows),
            outs[kv].at[:, half(h)],
            s_send.at[4 + t],
            s_recv.at[4 + t],
            before,
        ).start()

    for c in range(6):
        relay_b(c)
    for c in (0, 1):
        relay_c(c)
    for c in (6, 7):
        relay_b(c)
    for c in (0, 1):
        pass_on(c)
    for c in (0, 1):
        span_ready(c)
    lax.fori_loop(0, half_heads, backward, 0)
    send_near(0)
    send_queries(0)
    for c in (2, 3):
        relay_c(c)
    for c in (2, 3):
        pass_on(c)
    for t in (0, 1):
        send_far(t)
    for c in (2, 3):
        span_ready(c)
    lax.fori_loop(half_heads, kv_heads, backward, 0)
    send_near(1)
    send_queries(1)
    for t in (0, 1):
        relay_back_b(t)
    for t in (2, 3):
        send_far(t)
    for t in (2, 3):
        relay_back_b(t)
    for c in (4, 5):
        relay_c(c)
    for c in (6, 7):
        relay_c(c)
    turn(0)
    for c in (4, 5):
        pass_on(c)
    for c in (4, 5):
        span_ready(c)
    lax.fori_loop(0, half_heads, forward, 0)
    send_attended(0)
    for t in (0, 1):
        finish_near(t)
    for t in (0, 1):
        relay_back_c(t)
    for c in (6, 7):
        pass_on(c)
    for c in (6, 7):
        span_ready(c)
    lax.fori_loop(half_heads, kv_heads, forward, 0)
    send_attended(1)
    for t in (2, 3):
        finish_near(t)
    turn(1)
    for t in (2, 3):
        relay_back_c(t)
    for t in range(4):
        finish_across(t)

    for c in range(len(CHUNKS)):

        @pl.when(crossing)
        def _():
            for q in range(last):
                sent(source(c, piece(q)), a_send.at[c, q])

        @pl.when(has_next)
        def _():
            sent(rel_a.at[c], b_send.at[c])

        @pl.when(y < last)
        def _():
            sent(source(c, all_rows), r_send.at[c])

        @pl.when((y > 0) & has_prev)
        def _():
            sent(rel_b.at[c], c_send.at[c])

        @pl.when((core == 0) | (me >= 2))
        def _():
            sent(source(c, all_rows), e_send.at[c])

    for t in range(len(TERMS)):
        sent(terms_at(near, t, all_rows), f_send.at[t])

        @pl.when(y > 0)
        def _():
            sent(terms_at(far, t, all_rows), g_send.at[t])

        @pl.when(back_crossing)
        def _():
            for q in range(1, COLUMNS):
                sent(terms_at(far, t, piece(q)), ba_send.at[t, q])

        @pl.when(has_prev)
        def _():
            sent(back_a.at[t], bb_send.at[t])

        @pl.when((y < last) & has_next)
        def _():
            sent(back_b.at[t], bc_send.at[t])

    @pl.when(corner)
    def _():
        for h in range(2):
            sent(turned.at[h], t_send.at[h])

    moved = [(q_half(att, h), q_half(att_out, h)) for h in range(2)]
    moved += [(q_half(dq, h), q_half(dq_out, h)) for h in range(2)]
    moved += [(terms_at(final, t, all_rows), outs[t % 2].at[:, half(t // 2)]) for t in range(4)]
    for i, (src, dst) in enumerate(moved):
        sent(src, s_send.at[i])
        arrived(dst, s_recv.at[i])


def shards(tops, sections, queries, keys, values, out_grad, segments):
    q_width = queries.shape[-1]
    k_width = keys.shape[-1]
    kv_heads = k_width // HEAD_DIM
    half, full = jnp.bfloat16, jnp.float32
    vmem = pl.BlockSpec(memory_space=pltpu.VMEM)
    hbm = pl.BlockSpec(memory_space=pl.ANY)
    dma = pltpu.SemaphoreType.DMA
    results = pl.pallas_call(
        functools.partial(kernel, tops, sections, kv_heads),
        out_shape=[
            pltpu.VMEM((ROWS, q_width), half),
            pltpu.VMEM((ROWS, q_width), half),
            pltpu.VMEM((ROWS, k_width), half),
            pltpu.VMEM((ROWS, k_width), half),
        ],
        in_specs=[vmem, hbm, hbm, vmem, vmem],
        out_specs=[hbm] * 4,
        scratch_shapes=[
            pltpu.VMEM((2, 2, WINDOW + ROWS, k_width), half),
            pltpu.VMEM((2, WINDOW + ROWS, 2 * ROWS), full),
            pltpu.VMEM((ROWS, q_width), half),
            pltpu.VMEM((ROWS, q_width), half),
            pltpu.VMEM((2, ROWS, k_width), half),
            pltpu.VMEM((2, ROWS, k_width), half),
            pltpu.VMEM((2, ROWS, k_width), full),
            pltpu.VMEM((2, ROWS, k_width), half),
            pltpu.VMEM((2, ROWS, k_width), half),
            pltpu.VMEM((2, ROWS, k_width), half),
            pltpu.VMEM((8, PIECE, k_width // 2), half),
            pltpu.VMEM((8, PIECE, k_width // 2), half),
            pltpu.VMEM((4, PIECE, k_width // 2), half),
            pltpu.VMEM((4, PIECE, k_width // 2), half),
            dma((4,)),
            dma((8,)),
            dma((8,)),
            dma((8, COLUMNS)),
            dma((8,)),
            dma((8,)),
            dma((8,)),
            dma((8,)),
            dma((8, COLUMNS)),
            dma((8,)),
            dma((8,)),
            dma((4,)),
            dma((4,)),
            dma((4,)),
            dma((4,)),
            dma((4, COLUMNS)),
            dma((4,)),
            dma((4,)),
            dma((4,)),
            dma((4,)),
            dma((4, COLUMNS)),
            dma((8,)),
            dma((8,)),
            pltpu.VMEM((2, ROWS, q_width // 2), half),
            dma((2,)),
            dma((2,)),
        ],
        compiler_params=pltpu.CompilerParams(collective_id=0, has_side_effects=True),
    )(queries[0], keys[0], values[0], out_grad[0], segments)
    return tuple(result[None] for result in results)


def solution(mesh):
    tops = mesh.shape["seq"] // (2 * COLUMNS)
    sections = mesh.shape["section"]
    return jax.shard_map(
        functools.partial(shards, tops, sections),
        mesh=mesh,
        in_specs=(
            P("section", None, "seq", None),
            P("section", None, "seq", None),
            P("section", None, "seq", None),
            P("section", "seq", None),
            P(),
        ),
        out_specs=(
            P("section", "seq", None),
            P("section", "seq", None),
            P("section", "seq", None),
            P("section", "seq", None),
        ),
        check_vma=False,
    )
```
